32 devices in a mesh: shard: 2 (over y), ctx: 4 (over z), tp: 4 (over x, core).
Axes of the slice: x: 2, y: 2, z: 4, core: 2. Of those that a mesh axis runs over, the one named last changes fastest.
Arguments:
- inputs: bfloat16 [4, 1024, 768], P('shard', ('ctx', 'tp')), may hold values from -6 to 6
- seg_ids: int32 [4, 1024], P('shard', 'ctx'), may hold values from 0 to 7, never falling along the last dimension, each value on 1 to 512 neighbouring positions
- feature_map: float32 [12, 64, 256], P('tp'), may hold values from -6 to 6
- w_query: bfloat16 [768, 768], P(('shard', 'ctx'), 'tp'), may hold values from -0.21875 to 0.21875
- w_key: bfloat16 [768, 768], P(('shard', 'ctx'), 'tp'), may hold values from -0.21875 to 0.21875
- w_value: bfloat16 [768, 768], P(('shard', 'ctx'), 'tp'), may hold values from -0.21875 to 0.21875
- w_out: bfloat16 [768, 768], P('tp', ('shard', 'ctx')), may hold values from -0.875 to 0.875
- gain_attn: float32 [768], replicated, may hold values from 0.5 to 1.5
- shift_attn: float32 [768], replicated, may hold values from -3 to 3
- w_up: bfloat16 [768, 3072], P(('shard', 'ctx'), 'tp'), may hold values from -0.21875 to 0.21875
- bias_up: float32 [3072], P('tp'), may hold values from -3 to 3
- w_down: bfloat16 [3072, 768], P('tp', ('shard', 'ctx')), may hold values from -0.109375 to 0.109375
- bias_down: float32 [768], replicated, may hold values from -3 to 3
- gain_ffn: float32 [768], replicated, may hold values from 0.5 to 1.5
- shift_ffn: float32 [768], replicated, may hold values from -3 to 3
- cotangent: bfloat16 [4, 1024, 768], P('shard', ('ctx', 'tp')), may hold values from -6 to 6
Outputs:
- outputs: bfloat16 [4, 1024, 768], P('shard', ('ctx', 'tp'))
- grad_inputs: bfloat16 [4, 1024, 768], P('shard', ('ctx', 'tp'))
- grad_query: float32 [768, 768], P(('shard', 'ctx'), 'tp')
- grad_key: float32 [768, 768], P(('shard', 'ctx'), 'tp')
- grad_value: float32 [768, 768], P(('shard', 'ctx'), 'tp')
- grad_out: float32 [768, 768], P('tp', ('shard', 'ctx'))
- grad_gain_attn: float32 [768], replicated
- grad_shift_attn: float32 [768], replicated
- grad_up: float32 [768, 3072], P(('shard', 'ctx'), 'tp')
- grad_bias_up: float32 [3072], P('tp')
- grad_down: float32 [3072, 768], P('tp', ('shard', 'ctx'))
- grad_bias_down: float32 [768], replicated
- grad_gain_ffn: float32 [768], replicated
- grad_shift_ffn: float32 [768], replicated
The draws below stay inside these ranges and needn't reach their ends.
Inputs may be any that keep to these rules, and one draw needn't show every extreme that they name: `seg_ids`: within each sequence the numbers never fall, every number below 8 occurs, and no document has more than 512 tokens.
All inputs are finite; a program needn't handle non-finite values.
Results may differ from the reference program's by a relative error of at most 0.025.
Values may be sent and summed in bfloat16 or wider, within the bound.
A program may use at most 128 MiB of HBM per device.

```python
import math
import jax
import jax.numpy as jnp
import numpy as np
from jax import lax

D = 768
HEADS = 12
HEAD_DIM = 64
FEATS = 256
FF = 3072
LEN = 1024
SEQS = 4
SEGS = 8
SEG_MOST = 512


def steps_of(stream_key, dims, split, smallest, top_value):
    loudness, own = 1.0, jax.random.fold_in(stream_key, 6)
    for axis_at, parts in split:
        draws = jnp.exp(jax.random.uniform(jax.random.fold_in(own, axis_at), (parts,), jnp.float32, smallest / len(split), top_value / len(split)))
        loudness = loudness * jnp.repeat(draws, dims[axis_at] // parts).reshape([-1 if axis == axis_at else 1 for axis in range(len(dims))])
    return loudness


def split_up(count, total, limit, skew):
    loads = [(1 << 20) // math.isqrt(standing ** skew) + 1 for standing in range(2, count + 1)]
    spare, given = total - limit - (count - 1), [1] * (count - 1)
    while spare > 0:
        movable = [i for i in range(count - 1) if given[i] < limit]
        whole, left = sum([loads[i] for i in movable]), spare
        for i in movable:
            extra = min(limit - given[i], max(1, left * loads[i] // whole), spare)
            given[i] = given[i] + extra
            spare = spare - extra
    return np.array([limit] + given)


def uneven_parts(key, count, total, limit, lean):
    if count == 2:
        one = jax.random.randint(key, (), max(1, total - limit), min(limit, total - 1) + 1)
        return jnp.stack([one, total - one])
    lengths = jnp.asarray(split_up(count, total, limit, lean), jnp.int32)
    pairs = (count - 1) // 2
    donor, receiver = lengths[1:1 + 2 * pairs:2], lengths[2:2 + 2 * pairs:2]
    margin = jnp.minimum(donor - 1, limit - receiver)
    passed = jax.random.randint(jax.random.fold_in(key, 1), (pairs,), 0, 1 << 20) % (margin + 1)
    lengths = lengths.at[1:1 + 2 * pairs:2].set(donor - passed).at[2:2 + 2 * pairs:2].set(receiver + passed)
    return lengths[jax.random.permutation(jax.random.fold_in(key, 2), count)]


def scatter_about(rng, dims, scale, reach, shards=(), kind=jnp.bfloat16):
    factor_of = steps_of(rng, dims, shards, -0.22, 0.18) if shards else 1.0
    result = jax.random.normal(rng, dims, jnp.float32) * scale * factor_of
    return jnp.minimum(jnp.maximum(result, -reach), reach).astype(kind)


def setup_inputs(seed: int = 0) -> dict:
    keys = jax.random.split(jax.random.key(seed), 17)
    inputs = scatter_about(keys[0], (SEQS, LEN, D), 1.0, 6.0, ((0, 2), (1, 16)))
    seg_ids = jax.vmap(lambda own: jnp.searchsorted(jnp.cumsum(uneven_parts(own, SEGS, LEN, SEG_MOST, 2)), jnp.arange(LEN), side="right"))(jax.random.split(keys[1], SEQS)).reshape((SEQS, LEN)).astype(jnp.int32)
    feature_map = scatter_about(keys[2], (HEADS, HEAD_DIM, FEATS), 1.0, 6.0, ((0, 4),), jnp.float32)
    w_query = scatter_about(keys[3], (D, D), D ** -0.5, 0.21875, ((0, 8), (1, 4)))
    w_key = scatter_about(keys[4], (D, D), D ** -0.5, 0.21875, ((0, 8), (1, 4)))
    w_value = scatter_about(keys[5], (D, D), D ** -0.5, 0.21875, ((0, 8), (1, 4)))
    w_out = scatter_about(keys[6], (D, D), (D // 16) ** -0.5, 0.875, ((0, 4), (1, 8)))
    gain_attn = jnp.clip(1.0 + 0.1 * jax.random.normal(keys[7], (D,), jnp.float32), 0.5, 1.5)
    shift_attn = scatter_about(keys[8], (D,), 0.5, 3.0, (), jnp.float32)
    w_up = scatter_about(keys[9], (D, FF), D ** -0.5, 0.21875, ((0, 8), (1, 4)))
    bias_up = scatter_about(keys[10], (FF,), 0.5, 3.0, ((0, 4),), jnp.float32)
    w_down = scatter_about(keys[11], (FF, D), FF ** -0.5, 0.109375, ((0, 4), (1, 8)))
    bias_down = scatter_about(keys[12], (D,), 0.5, 3.0, (), jnp.float32)
    gain_ffn = jnp.clip(1.0 + 0.1 * jax.random.normal(keys[13], (D,), jnp.float32), 0.5, 1.5)
    shift_ffn = scatter_about(keys[14], (D,), 0.5, 3.0, (), jnp.float32)
    cotangent = scatter_about(keys[15], (SEQS, LEN, D), 1.0, 6.0, ((0, 2), (1, 16)))
    return {"inputs": inputs, "seg_ids": seg_ids, "feature_map": feature_map, "w_query": w_query, "w_key": w_key, "w_value": w_value, "w_out": w_out, "gain_attn": gain_attn, "shift_attn": shift_attn, "w_up": w_up, "bias_up": bias_up, "w_down": w_down, "bias_down": bias_down, "gain_ffn": gain_ffn, "shift_ffn": shift_ffn, "cotangent": cotangent}


highest = lax.Precision.HIGHEST
root_half = 0.7071067811865476
norm_eps = 1e-05

@jax.custom_vjp
def low(v):
    return lax.optimization_barrier(v.astype(jnp.bfloat16)).astype(jnp.float32)

@jax.custom_vjp
def low_back(v):
    return v

def low_keep(v):
    return (low(v), None)

def low_pass(kept, grad):
    return (grad,)

def back_keep(v):
    return (v, None)

def back_low(kept, grad):
    return (low(grad),)
low.defvjp(low_keep, low_pass)
low_back.defvjp(back_keep, back_low)

def gelu_value(upper):
    return upper * 0.5 * (1.0 + lax.erf(upper * root_half))

def layer_norm(hidden_in, gain_vec, shift_vec):
    mean_val = lax.optimization_barrier(jnp.mean(hidden_in, -1, keepdims=True))
    centred = hidden_in - mean_val
    inv_std = lax.rsqrt(lax.optimization_barrier(jnp.mean(centred * centred, -1, keepdims=True)) + norm_eps)
    return centred * inv_std * gain_vec + shift_vec

def phi_map(heads_in, omega_head):
    scaled = heads_in * HEAD_DIM ** (-0.25)
    angles = jnp.einsum('sjd,dm->sjm', scaled, omega_head, precision=highest)
    return jnp.exp(angles - 0.5 * lax.optimization_barrier(jnp.sum(scaled * scaled, -1, keepdims=True))) * FEATS ** (-0.5)

def block_forward(inputs_f, weight_set, seg_block, feature_map):
    w_query, w_key, w_value, w_out, gain_attn, shift_attn, w_up, bias_up, w_down, bias_down, gain_ffn, shift_ffn = weight_set
    seq_count = inputs_f.shape[0]
    flat = inputs_f.reshape(-1, D)

    def project(weight):
        made = jnp.dot(flat, weight, precision=highest)
        return made.reshape(seq_count, LEN, HEADS, HEAD_DIM).transpose(2, 0, 1, 3)
    query_heads = low_back(project(w_query))
    key_heads = low_back(project(w_key))
    value_heads = low(low_back(project(w_value)))
    mask = (seg_block[:, :, None] == jnp.arange(SEGS, dtype=jnp.int32)).astype(jnp.float32)

    def one_head(operands):
        query_h, key_h, value_h, omega_h = operands
        phi_query = low(phi_map(query_h, omega_h))
        phi_key = low(phi_map(key_h, omega_h))
        wide_key = (mask[:, :, :, None] * phi_key[:, :, None, :]).reshape(seq_count, LEN, -1)
        table = low(low_back(jnp.einsum('sjx,sje->sxe', wide_key, value_h, precision=highest)))
        normal_sum = jnp.einsum('sjg,sjm->sgm', mask, phi_key, precision=highest)
        wide_query = (mask[:, :, :, None] * phi_query[:, :, None, :]).reshape(seq_count, LEN, -1)
        numer = low_back(jnp.einsum('sjx,sxe->sje', wide_query, table, precision=highest))
        denom = lax.optimization_barrier(jnp.sum(jnp.einsum('sjm,sgm->sjg', phi_query, normal_sum, precision=highest) * mask, -1))
        return numer / denom[..., None]
    heads_out = lax.map(jax.checkpoint(one_head), (query_heads, key_heads, value_heads, feature_map))
    mixed = heads_out.transpose(1, 2, 0, 3).reshape(-1, D)
    attn = low_back(jnp.dot(low(mixed), w_out, precision=highest))
    first = layer_norm(flat + attn, gain_attn, shift_attn)
    upper = low_back(jnp.dot(low(first), w_up, precision=highest) + bias_up)
    branch = low_back(jnp.dot(low(gelu_value(upper)), w_down, precision=highest))
    final = layer_norm(first + branch + bias_down, gain_ffn, shift_ffn)
    return final.reshape(seq_count, LEN, D)

def reference(inputs, seg_ids, feature_map, w_query, w_key, w_value, w_out, gain_attn, shift_attn, w_up, bias_up, w_down, bias_down, gain_ffn, shift_ffn, cotangent):
    weight_set = (w_query.astype(jnp.float32), w_key.astype(jnp.float32), w_value.astype(jnp.float32), w_out.astype(jnp.float32), gain_attn.astype(jnp.float32), shift_attn.astype(jnp.float32), w_up.astype(jnp.float32), bias_up.astype(jnp.float32), w_down.astype(jnp.float32), bias_down.astype(jnp.float32), gain_ffn.astype(jnp.float32), shift_ffn.astype(jnp.float32))
    omega_all = feature_map.astype(jnp.float32)
    group_size = 4 if SEQS % 4 == 0 else 2 if SEQS % 2 == 0 else 1
    blocks = SEQS // group_size
    inputs_b = inputs.astype(jnp.float32).reshape(blocks, group_size, LEN, D)
    cot_b = cotangent.astype(jnp.float32).reshape(blocks, group_size, LEN, D)
    seg_b = seg_ids.astype(jnp.int32).reshape(blocks, group_size, LEN)
    zeros_set = jax.tree.map(jnp.zeros_like, weight_set)

    def step_fn(carry, operands):
        inputs_g, seg_g, cot_g = operands
        value_out, pullback = jax.vjp(lambda data_in, weight_in: block_forward(data_in, weight_in, seg_g, omega_all), inputs_g, weight_set)
        grad_data, grad_weights = pullback(cot_g)
        return (jax.tree.map(jnp.add, carry, grad_weights), (value_out, grad_data))
    totals, (values_all, grads_all) = lax.scan(step_fn, zeros_set, (inputs_b, seg_b, cot_b))
    outputs = values_all.reshape(SEQS, LEN, D).astype(jnp.bfloat16)
    grad_inputs = grads_all.reshape(SEQS, LEN, D).astype(jnp.bfloat16)
    grad_query, grad_key, grad_value, grad_out, grad_gain_attn, grad_shift_attn, grad_up, grad_bias_up, grad_down, grad_bias_down, grad_gain_ffn, grad_shift_ffn = totals
    return (outputs, grad_inputs, grad_query, grad_key, grad_value, grad_out, grad_gain_attn, grad_shift_attn, grad_up, grad_bias_up, grad_down, grad_bias_down, grad_gain_ffn, grad_shift_ffn)
```

```python
import jax
import jax.numpy as jnp
from jax import lax
from jax.experimental import pallas as pl
from jax.experimental.pallas import tpu as pltpu
from jax.sharding import PartitionSpec as P

HEAD_DIM = 64
FEATS = 256
FF = 3072
SEGS = 8


highest = lax.Precision.HIGHEST
root_half = 0.7071067811865476
inv_root_tau = 0.3989422804014327
norm_eps = 1e-05


def gelu_value(upper):
    return upper * 0.5 * (1.0 + lax.erf(upper * root_half))


def gelu_slope(upper):
    return 0.5 * (1.0 + lax.erf(upper * root_half)) + upper * inv_root_tau * jnp.exp(
        -0.5 * upper * upper
    )


def layer_norm(hidden_in, gain_vec, shift_vec):
    mean_val = jnp.mean(hidden_in, -1, keepdims=True)
    centred = hidden_in - mean_val
    inv_std = lax.rsqrt(jnp.mean(centred * centred, -1, keepdims=True) + norm_eps)
    normed = centred * inv_std
    return (normed * gain_vec + shift_vec, normed, inv_std)


def norm_back(grad_in, normed, inv_std, gain_vec):
    scaled = grad_in * gain_vec
    grad_hidden = inv_std * (
        scaled
        - jnp.mean(scaled, -1, keepdims=True)
        - normed * jnp.mean(scaled * normed, -1, keepdims=True)
    )
    return (grad_hidden, jnp.sum(grad_in * normed, (0, 1)), jnp.sum(grad_in, (0, 1)))


def features(projected, omega_local):
    seq_count, ctx_rows, width = projected.shape
    heads_here = omega_local.shape[0]
    scaled = projected.reshape(seq_count, ctx_rows, heads_here, HEAD_DIM) * HEAD_DIM ** (-0.25)
    angles = jnp.einsum("schd,hdm->schm", scaled, omega_local, precision=highest)
    squares = 0.5 * jnp.sum(scaled * scaled, -1, keepdims=True)
    return (jnp.exp(angles - squares) * FEATS ** (-0.5), scaled)


def feature_back(grad_phi, phi_full, scaled, omega_local):
    grad_angle = grad_phi * phi_full
    grad_scaled = jnp.einsum("schm,hdm->schd", grad_angle, omega_local, precision=highest)
    grad_scaled = grad_scaled - scaled * jnp.sum(grad_angle, -1, keepdims=True)
    seq_count, ctx_rows, heads_here, head_width = scaled.shape
    return (grad_scaled * HEAD_DIM ** (-0.25)).reshape(seq_count, ctx_rows, heads_here * head_width)


def spread_rows(mask_low, left):
    ctx_rows, heads_here, feat_count = left.shape
    wide = mask_low[:, None, :, None] * left[:, :, None, :]
    return wide.reshape(ctx_rows, heads_here, -1)


def segment_outer(operands):
    mask_low, left, right = operands
    return jnp.einsum(
        "chx,che->hxe", spread_rows(mask_low, left), right, preferred_element_type=jnp.float32
    )


def segment_apply(operands):
    mask_low, left, table = operands
    return jnp.einsum(
        "chx,hxe->che", spread_rows(mask_low, left), table, preferred_element_type=jnp.float32
    )


def segment_back(operands):
    mask_full, left, table = operands
    ctx_rows, heads_here, width = left.shape
    seg_count = mask_full.shape[1]
    wide = jnp.einsum("che,hxe->chx", left, table, preferred_element_type=jnp.float32)
    wide = wide.reshape(ctx_rows, heads_here, seg_count, -1)
    return jnp.sum(wide * mask_full[:, None, :, None], 2)


def inner_product(left, right):
    return lax.dot_general(
        left, right, (((0,), (0,)), ((), ())), preferred_element_type=jnp.float32
    )


def right_transposed(left, right):
    return lax.dot_general(
        left, right, (((1,), (1,)), ((), ())), preferred_element_type=jnp.float32
    )


def per_device(
    inputs,
    seg_ids,
    feature_map,
    w_query,
    w_key,
    w_value,
    w_out,
    gain_attn,
    shift_attn,
    w_up,
    bias_up,
    w_down,
    bias_down,
    gain_ffn,
    shift_ffn,
    cotangent,
):
    full_query, full_key, full_value, full_up, full_out, full_down = (
        lax.all_gather(w_query, ("shard", "ctx"), axis=0, tiled=True),
        lax.all_gather(w_key, ("shard", "ctx"), axis=0, tiled=True),
        lax.all_gather(w_value, ("shard", "ctx"), axis=0, tiled=True),
        lax.all_gather(w_up, ("shard", "ctx"), axis=0, tiled=True),
        lax.all_gather(w_out, ("shard", "ctx"), axis=1, tiled=True),
        lax.all_gather(w_down, ("shard", "ctx"), axis=1, tiled=True),
    )
    seq_count, row_share, width = inputs.shape
    rows_all = lax.all_gather(inputs, "tp", axis=1, tiled=True)
    ctx_rows = rows_all.shape[1]
    token_count = seq_count * ctx_rows
    flat = rows_all.reshape(token_count, width)
    heads_here = feature_map.shape[0]
    head_cols = heads_here * HEAD_DIM
    query_proj = jnp.dot(flat, full_query, preferred_element_type=jnp.float32).reshape(
        seq_count, ctx_rows, head_cols
    )
    key_proj = jnp.dot(flat, full_key, preferred_element_type=jnp.float32).reshape(
        seq_count, ctx_rows, head_cols
    )
    value_low = jnp.dot(flat, full_value, preferred_element_type=jnp.float32).astype(jnp.bfloat16)
    value_low = value_low.reshape(seq_count, ctx_rows, head_cols)
    value_four = value_low.reshape(seq_count, ctx_rows, heads_here, HEAD_DIM)
    phi_query, scaled_query = features(query_proj, feature_map)
    phi_key, scaled_key = features(key_proj, feature_map)
    phq_low = phi_query.astype(jnp.bfloat16)
    phk_low = phi_key.astype(jnp.bfloat16)
    matches = seg_ids[:, :, None] == jnp.arange(SEGS, dtype=jnp.int32)[None, None, :]
    mask_low = matches.astype(jnp.bfloat16)
    mask_full = matches.astype(jnp.float32)
    kv_part = lax.map(segment_outer, (mask_low, phk_low, value_four))
    z_part = jnp.einsum("scg,schm->shgm", mask_low, phk_low, preferred_element_type=jnp.float32)
    kv_sum, z_sum = lax.psum((kv_part, z_part), "ctx")
    kv_low = kv_sum.astype(jnp.bfloat16)
    numer = lax.map(segment_apply, (mask_low, phq_low, kv_low))
    phq_wide = phq_low.astype(jnp.float32)
    denom = jnp.sum(
        jnp.einsum("schm,shgm->schg", phq_wide, z_sum, precision=highest)
        * mask_full[:, :, None, :],
        -1,
    )
    mixed = numer / denom[..., None]
    mixed_low = mixed.astype(jnp.bfloat16).reshape(seq_count, ctx_rows, head_cols)
    piece = mixed_low
    attn_sum = jnp.swapaxes(
        lax.psum_scatter(
            jnp.einsum("scf,fd->csd", piece, full_out, preferred_element_type=jnp.float32),
            "tp",
            scatter_dimension=0,
            tiled=True,
        ),
        0,
        1,
    )
    first, normed_one, inv_one = layer_norm(
        inputs.astype(jnp.float32) + attn_sum, gain_attn, shift_attn
    )
    first_low = first.astype(jnp.bfloat16)
    first_rows = lax.all_gather(first_low, "tp", axis=1, tiled=True)
    first_flat = first_rows.reshape(token_count, width)
    upper = jnp.dot(first_flat, full_up, preferred_element_type=jnp.float32) + bias_up
    ffn_here = upper.shape[1]
    hidden_low = gelu_value(upper).astype(jnp.bfloat16)
    hidden_three = hidden_low.reshape(seq_count, ctx_rows, ffn_here)
    piece = hidden_three
    branch = jnp.swapaxes(
        lax.psum_scatter(
            jnp.einsum("scf,fd->csd", piece, full_down, preferred_element_type=jnp.float32),
            "tp",
            scatter_dimension=0,
            tiled=True,
        ),
        0,
        1,
    )
    final, normed_two, inv_two = layer_norm(first + branch + bias_down, gain_ffn, shift_ffn)
    outputs = final.astype(jnp.bfloat16)
    full_query, full_key, full_value, full_up, full_out, full_down = (
        lax.all_gather(w_query, ("shard", "ctx"), axis=0, tiled=True),
        lax.all_gather(w_key, ("shard", "ctx"), axis=0, tiled=True),
        lax.all_gather(w_value, ("shard", "ctx"), axis=0, tiled=True),
        lax.all_gather(w_up, ("shard", "ctx"), axis=0, tiled=True),
        lax.all_gather(w_out, ("shard", "ctx"), axis=1, tiled=True),
        lax.all_gather(w_down, ("shard", "ctx"), axis=1, tiled=True),
    )
    grad_final = cotangent.astype(jnp.float32)
    grad_two, grad_gain_ffn, grad_shift_ffn = norm_back(grad_final, normed_two, inv_two, gain_ffn)
    grad_bias_down = jnp.sum(grad_two, (0, 1))
    grad_two_rows = lax.all_gather(grad_two.astype(jnp.bfloat16), "tp", axis=1, tiled=True)
    grad_two_flat = grad_two_rows.reshape(token_count, width)
    grad_hidden = right_transposed(grad_two_flat, full_down)
    grad_upper = (grad_hidden * gelu_slope(upper)).astype(jnp.bfloat16)
    grad_down = inner_product(hidden_low, grad_two_flat)
    grad_up = inner_product(first_flat, grad_upper)
    grad_bias_local = jnp.sum(grad_upper.astype(jnp.float32), 0)
    grad_upper_three = grad_upper.reshape(seq_count, ctx_rows, ffn_here)
    piece = grad_upper_three
    grad_first = grad_two + jnp.swapaxes(
        lax.psum_scatter(
            jnp.einsum("scf,df->csd", piece, full_up, preferred_element_type=jnp.float32),
            "tp",
            scatter_dimension=0,
            tiled=True,
        ),
        0,
        1,
    )
    grad_one, grad_gain_attn, grad_shift_attn = norm_back(
        grad_first, normed_one, inv_one, gain_attn
    )
    grad_one_rows = lax.all_gather(grad_one.astype(jnp.bfloat16), "tp", axis=1, tiled=True)
    grad_one_flat = grad_one_rows.reshape(token_count, width)
    grad_out = inner_product(mixed_low.reshape(token_count, head_cols), grad_one_flat)
    grad_mixed = right_transposed(grad_one_flat, full_out).reshape(
        seq_count, ctx_rows, heads_here, HEAD_DIM
    )
    grad_numer = (grad_mixed / denom[..., None]).astype(jnp.bfloat16)
    grad_denom = -jnp.sum(grad_mixed * mixed, -1) / denom
    kv_grad_part = lax.map(segment_outer, (mask_low, phq_low, grad_numer))
    z_grad_part = jnp.einsum(
        "scg,schm->shgm", mask_full, phq_wide * grad_denom[..., None], precision=highest
    )
    kv_grad, z_grad = (
        lax.psum(kv_grad_part.astype(jnp.bfloat16), "ctx").astype(jnp.float32),
        lax.psum(z_grad_part.astype(jnp.bfloat16), "ctx").astype(jnp.float32),
    )
    kv_grad_low = kv_grad.astype(jnp.bfloat16)
    grad_phq = lax.map(segment_back, (mask_full, grad_numer, kv_low))
    grad_phq = grad_phq + grad_denom[..., None] * jnp.einsum(
        "scg,shgm->schm", mask_full, z_sum, precision=highest
    )
    grad_phk = lax.map(segment_back, (mask_full, value_four, kv_grad_low))
    grad_phk = grad_phk + jnp.einsum("scg,shgm->schm", mask_full, z_grad, precision=highest)
    grad_value_rows = lax.map(segment_apply, (mask_low, phk_low, kv_grad_low)).astype(jnp.bfloat16)
    grad_value_rows = grad_value_rows.reshape(seq_count, ctx_rows, head_cols)
    grad_query_rows = feature_back(grad_phq, phi_query, scaled_query, feature_map).astype(
        jnp.bfloat16
    )
    grad_key_rows = feature_back(grad_phk, phi_key, scaled_key, feature_map).astype(jnp.bfloat16)
    grad_query = inner_product(flat, grad_query_rows.reshape(token_count, head_cols))
    grad_key = inner_product(flat, grad_key_rows.reshape(token_count, head_cols))
    grad_value = inner_product(flat, grad_value_rows.reshape(token_count, head_cols))
    total = jnp.einsum(
        "scf,df->csd", grad_query_rows, full_query, preferred_element_type=jnp.float32
    )
    total = total + jnp.einsum(
        "scf,df->csd", grad_key_rows, full_key, preferred_element_type=jnp.float32
    )
    grad_rows = jnp.swapaxes(
        lax.psum_scatter(
            (
                total
                + jnp.einsum(
                    "scf,df->csd", grad_value_rows, full_value, preferred_element_type=jnp.float32
                )
            ).astype(jnp.bfloat16),
            "tp",
            scatter_dimension=0,
            tiled=True,
        ).astype(jnp.float32),
        0,
        1,
    )
    grad_inputs = (grad_one + grad_rows).astype(jnp.bfloat16)
    grad_query, grad_key, grad_value, grad_up, grad_out, grad_down = (
        lax.psum_scatter(grad_query, ("shard", "ctx"), scatter_dimension=0, tiled=True),
        lax.psum_scatter(grad_key, ("shard", "ctx"), scatter_dimension=0, tiled=True),
        lax.psum_scatter(grad_value, ("shard", "ctx"), scatter_dimension=0, tiled=True),
        lax.psum_scatter(grad_up, ("shard", "ctx"), scatter_dimension=0, tiled=True),
        lax.psum_scatter(grad_out, ("shard", "ctx"), scatter_dimension=1, tiled=True),
        lax.psum_scatter(grad_down, ("shard", "ctx"), scatter_dimension=1, tiled=True),
    )
    tp_index = lax.axis_index("tp")
    padded_bias = lax.dynamic_update_slice(
        jnp.zeros((FF,), jnp.float32), grad_bias_local, (tp_index * ffn_here,)
    )
    grad_gain_attn, grad_shift_attn, grad_gain_ffn, grad_shift_ffn, grad_bias_down, padded_bias = (
        lax.psum(
            (
                grad_gain_attn,
                grad_shift_attn,
                grad_gain_ffn,
                grad_shift_ffn,
                grad_bias_down,
                padded_bias,
            ),
            ("shard", "ctx", "tp"),
        )
    )
    grad_bias_up = lax.dynamic_slice(padded_bias, (tp_index * ffn_here,), (ffn_here,))
    return (
        outputs,
        grad_inputs,
        grad_query,
        grad_key,
        grad_value,
        grad_out,
        grad_gain_attn,
        grad_shift_attn,
        grad_up,
        grad_bias_up,
        grad_down,
        grad_bias_down,
        grad_gain_ffn,
        grad_shift_ffn,
    )


BF = jnp.bfloat16
F32 = jnp.float32
MESH_ID = pl.DeviceIdType.MESH
TAB = 80
SUBS = 3


def nn(left, right):
    return lax.dot_general(left, right, (((1,), (0,)), ((), ())), preferred_element_type=F32)


def nt(left, right):
    return lax.dot_general(left, right, (((1,), (1,)), ((), ())), preferred_element_type=F32)


def tn(left, right):
    return lax.dot_general(left, right, (((0,), (0,)), ((), ())), preferred_element_type=F32)


def lanes_of(shape):
    return lax.broadcasted_iota(jnp.int32, shape, 1)


def norm_stats(hidden_in):
    centred = hidden_in - jnp.mean(hidden_in, -1, keepdims=True)
    inv_std = lax.rsqrt(jnp.mean(centred * centred, -1, keepdims=True) + norm_eps)
    return centred * inv_std, inv_std


def norm_grad(grad_in, normed, inv_std, gain_vec):
    scaled = grad_in * gain_vec
    return inv_std * (
        scaled
        - jnp.mean(scaled, -1, keepdims=True)
        - normed * jnp.mean(scaled * normed, -1, keepdims=True)
    )


def layer_kernel(
    x_ref, seg_ref, om_ref, wq_ref, wk_ref, wv_ref, wo_ref, ga_ref, sa_ref, wu_ref, bu_ref, wd_ref,
    bd_ref, gf_ref, sf_ref, cot_ref,
    out_ref, gin_ref, ok_ref, ov_ref, oq_ref, oo_ref, ou_ref, od_ref, small_ref,
    X, FI, G2, G1, WK, WV, WQ, WO, WU, WD, OWN_O, OWN_D, P, HID, SLOPE, GUP,
    FIRST, NORM1, INV1, GH2, GH1,
    RQ, RK, VX, PQF, PKF, PQ, PK, SS, MSK, CM, SEGZ,
    OM1, OM2, OMT,
    MIX, DEN, GX, GKL, GVL, GM, GM3, GV3, RGK, RGV, RGQ, MIXC,
    TBS, TBR, COMB, GCOMB,
    SIBS, SIBR, XS, XR,
    GON, GOW, YSN, YSW, YRN, YRW, ZSN, ZSW, ZRN, ZRW,
    ARS, ARR, ARZ,
    ag_s, ag_r, ra_s, ra_r, seg_s, seg_r, wz_s, wz_r, wy_s, wy_r, wc_s, wc_r, wf_s, wf_r, gy_s, gy_r, gz_s, gz_r, gc_s, gc_r, tb_s, tb_r, ar_s, ar_r,
):
    y = lax.axis_index("shard")
    z = lax.axis_index("ctx")
    t = lax.axis_index("tp")
    sib_t, far_t = t + 1 - 2 * (t % 2), 3 - t
    sib = {"tp": sib_t}
    far = {"tp": far_t}
    yp = {"shard": 1 - y}

    def along(d):
        return {"ctx": (z + d) % 4}

    def block_rows(yy, zz):
        return pl.ds(pl.multiple_of((yy * 4 + zz) * 96, 96), 96)

    def copy(src, dst, send, recv, where):
        return pltpu.make_async_remote_copy(
            src_ref=src, dst_ref=dst, send_sem=send, recv_sem=recv, device_id=where,
            device_id_type=MESH_ID,
        )

    barrier = pltpu.get_barrier_semaphore()
    for where in (sib, far, yp, along(1), along(2), along(3)):
        pl.semaphore_signal(barrier, inc=1, device_id=where, device_id_type=MESH_ID)
    pl.semaphore_wait(barrier, 6)

    def chunk(tt):
        return pl.ds(pl.multiple_of(tt * 64, 64), 64)

    def ag_desc(op, buf, s, which):
        rows = chunk(far_t) if which == 2 else chunk(t)
        where = far if which == 1 else sib
        return copy(
            buf.at[s, rows, :], buf.at[s, rows, :], ag_s.at[op, s, which], ag_r.at[op, s, which], where
        )

    def ag_start(op, buf, s):
        ag_desc(op, buf, s, 1).start()
        ag_desc(op, buf, s, 0).start()

    def ag_pass(op, buf, s):
        ag_desc(op, buf, s, 1).wait_recv()
        ag_desc(op, buf, s, 2).start()

    def ag_wait(op, buf, s):
        ag_desc(op, buf, s, 0).wait_recv()
        ag_desc(op, buf, s, 2).wait_recv()

    def sib_desc(op, s, part):
        return copy(
            SIBS.at[op, s, part], SIBR.at[op, s, part], ra_s.at[op, s, part], ra_r.at[op, s, part], sib
        )

    def xrs_desc(op, s):
        return copy(XS.at[op, s], XR.at[op, s], ra_s.at[op, s, 2], ra_r.at[op, s, 2], far)

    def part_rows(s, tt):
        return P[s, chunk(tt), :]

    def rs_start(op, s):
        SIBS[op, s, 0] = part_rows(s, (t + 2) % 4).astype(BF)
        sib_desc(op, s, 0).start()
        SIBS[op, s, 1] = part_rows(s, sib_t).astype(BF)
        sib_desc(op, s, 1).start()

    def rs_mid(op, s):
        sib_desc(op, s, 0).wait_recv()
        XS[op, s] = (part_rows(s, far_t) + SIBR[op, s, 0].astype(F32)).astype(BF)
        xrs_desc(op, s).start()

    def rs_fin(op, s):
        sib_desc(op, s, 1).wait_recv()
        kept = part_rows(s, t) + SIBR[op, s, 1].astype(F32)
        xrs_desc(op, s).wait_recv()
        return kept + XR[op, s].astype(F32)

    gathered = (WK, WV, WQ, WO, WU, WD)
    mine = (wk_ref, wv_ref, wq_ref, OWN_O, wu_ref, OWN_D)

    def wz_desc(i, d):
        dst = gathered[i].at[block_rows(y, z), :]
        return copy(mine[i], dst, wz_s.at[i, d - 1], wz_r.at[i, d - 1], along(d))

    def wy_desc(i, d):
        dst = gathered[i].at[block_rows(y, (z + 4 - d) % 4), :]
        return copy(mine[i] if d == 0 else dst, dst, wy_s.at[i, d], wy_r.at[i, d], yp)

    def step_of(way):
        return 1 - 2 * way

    def came(way, j):
        return z > j if way == 0 else z + j < 3

    def goes(way, j):
        return (z >= j) & (z < 3) if way == 0 else (z + j <= 3) & (z > 0)

    def wc_desc(i, way, j):
        dst = gathered[i].at[block_rows(y, (z + 4 - j * step_of(way)) % 4), :]
        src = mine[i] if j == 0 else dst
        return copy(src, dst, wc_s.at[i - 4, way, j], wc_r.at[i - 4, way, j], along(4 + step_of(way)))

    def wf_desc(i, way, j):
        part = gathered[i].at[block_rows(y, (z + 4 - (j + 1) * step_of(way)) % 4), :]
        return copy(part, part, wf_s.at[i - 4, way, j], wf_r.at[i - 4, way, j], yp)

    def w_send(i):
        if i < 4:
            for d in (2, 1, 3):
                wz_desc(i, d).start()
        else:
            for way in range(2):

                @pl.when(goes(way, 0))
                def _():
                    wc_desc(i, way, 0).start()

        wy_desc(i, 0).start()

    def w_pass(i):
        for d in (2, 1, 3):
            wz_desc(i, d).wait_recv()
            wy_desc(i, d).start()

    def w_relay(i, j):
        for way in range(2):

            @pl.when(came(way, j))
            def _():
                wc_desc(i, way, j).wait_recv()

            if j < 2:

                @pl.when(goes(way, j + 1))
                def _():
                    wc_desc(i, way, j + 1).start()

            @pl.when(came(way, j))
            def _():
                wf_desc(i, way, j).start()

    def w_wait(i):
        wy_desc(i, 0).wait_recv()
        if i < 4:
            for d in (1, 2, 3):
                wy_desc(i, d).wait_recv()
            return
        for way in range(2):
            for j in range(3):

                @pl.when(came(way, j))
                def _():
                    wf_desc(i, way, j).wait_recv()

    w_send(0)
    w_send(1)
    own = block_rows(y, z)
    for s in range(2):
        X[s, chunk(t), :] = x_ref[s]
        ag_start(0, X, s)
    w_send(2)
    TBR[...] = jnp.zeros_like(TBR)
    COMB[...] = jnp.zeros_like(COMB)
    GCOMB[...] = jnp.zeros_like(GCOMB)

    def seg_desc(d):
        return copy(seg_ref, SEGZ.at[z], seg_s.at[d - 1], seg_r.at[d - 1], along(d))

    for d in (1, 2, 3):
        seg_desc(d).start()
    WK[own, :] = wk_ref[...]
    WV[own, :] = wv_ref[...]
    WQ[own, :] = wq_ref[...]
    WU[own, :] = wu_ref[...]
    turned = wo_ref[...].T
    OWN_O[...] = turned
    WO[own, :] = turned
    turned = wd_ref[...].T
    OWN_D[...] = turned
    WD[own, :] = turned

    def split_omega(h, carry):
        om = om_ref[h]
        hi = om.astype(BF)
        low = (om - hi.astype(F32)).astype(BF)
        zero = jnp.zeros((64, 256), BF)
        OM1[h] = jnp.concatenate([hi, zero, hi, zero], axis=0)
        OM2[h] = jnp.concatenate([low, zero], axis=0)
        turned = jnp.concatenate([om, jnp.zeros((64, 256), F32)], axis=0).T
        t_hi = turned.astype(BF)
        t_low = (turned - t_hi.astype(F32)).astype(BF)
        one_at = (lanes_of((256, 128)) == 64).astype(BF)
        OMT[h] = jnp.concatenate([t_hi + one_at, t_low], axis=1)
        return carry

    lax.fori_loop(0, 3, split_omega, 0)

    for s in range(2):
        ag_pass(0, X, s)
    w_pass(0)
    w_pass(1)

    for d in (1, 2, 3):
        seg_desc(d).wait_recv()
    seg_row = [seg_ref[s : s + 1, :] for s in range(2)]

    def edge(s, side, dist):
        if side == 0:
            return SEGZ[(z + 4 - dist) % 4, s : s + 1, 255:256]
        return SEGZ[(z + dist) % 4, s : s + 1, 0:1]

    def reaches(side, dist):
        return z >= dist if side == 0 else z + dist <= 3

    for s in range(2):
        wide = jnp.broadcast_to(seg_row[s].astype(F32), (256, 256))
        col = wide.T
        MSK[s] = (wide == col).astype(F32)
        for side in range(2):
            near = (col[:, 0:128] == edge(s, side, 1).astype(F32)).astype(F32)
            CM[side, s] = jnp.where(reaches(side, 1), near, 0.0)

    def first_row(s):
        return (seg_row[s] == seg_row[s][:, 0:1]).astype(F32)

    def last_row(s):
        return (seg_row[s] == seg_row[s][:, 255:256]).astype(F32)

    def project_keys(s):
        rows = X[s]
        made_k = nn(rows, WK[...]) * HEAD_DIM ** (-0.25)
        made_v = nn(rows, WV[...])
        zero = jnp.zeros((256, 64), F32)
        lane = lanes_of((256, 128))
        for h in range(3):
            i = s * 3 + h
            RK[i] = jnp.concatenate([made_k[:, 64 * h : 64 * h + 64], zero], axis=1)
            v_h = jnp.concatenate([made_v[:, 64 * h : 64 * h + 64], zero], axis=1)
            VX[i] = jnp.where((lane == 64) | (lane == 65), 1.0, v_h).astype(BF)

    def project_queries(s):
        made_q = nn(X[s], WQ[...]) * HEAD_DIM ** (-0.25)
        zero = jnp.zeros((256, 64), F32)
        for h in range(3):
            RQ[s * 3 + h] = jnp.concatenate([made_q[:, 64 * h : 64 * h + 64], zero], axis=1)

    def phi_of(scaled, h):
        hi = scaled.astype(BF)
        low = (scaled - hi.astype(F32)).astype(BF)
        angles = nn(jnp.concatenate([hi, low], axis=1), OM1[h]) + nn(hi, OM2[h])
        squares = 0.5 * jnp.sum(scaled * scaled, -1, keepdims=True)
        return jnp.exp(angles - squares) * FEATS ** (-0.5)

    def tables(ext, feats, s):
        turned = ext.astype(F32).T[0:TAB, :]
        both = jnp.concatenate([turned * first_row(s), turned * last_row(s)], axis=0)
        return nn(both.astype(BF), feats)

    def keys(s):
        def body(h, carry):
            i = s * 3 + h
            phi = phi_of(RK[i], h)
            PKF[i] = phi
            low = phi.astype(BF)
            PK[i] = low
            made = tables(VX[i], low, s)
            TBS[0, 1, i] = made[0:TAB].astype(BF)
            TBS[0, 0, i] = made[TAB : 2 * TAB].astype(BF)
            return carry

        lax.fori_loop(0, 3, body, 0)

    def queries(s):
        def body(h, carry):
            i = s * 3 + h
            phi = phi_of(RQ[i], h)
            PQF[i] = phi
            low = phi.astype(BF)
            PQ[i] = low
            score = jnp.where(MSK[s] > 0, nt(low, PK[i]), 0.0).astype(BF)
            SS[i] = score
            MIX[i] = nn(score, VX[i])
            return carry

        lax.fori_loop(0, 3, body, 0)

    def mixing(s):
        tb_take(0, s, COMB)

        def body(h, carry):
            i = s * 3 + h
            cross = nt(PQ[i], COMB[i])
            numer = MIX[i] + jnp.where(CM[0, s] > 0, cross[:, 0:128], 0.0)
            numer = numer + jnp.where(CM[1, s] > 0, cross[:, 128:256], 0.0)
            denom = numer[:, 64:65]
            mixed = numer / denom
            MIX[i] = jnp.where(lanes_of((256, 128)) < 64, mixed, 0.0)
            DEN[i] = jnp.broadcast_to(denom, (256, 128))
            return carry

        lax.fori_loop(0, 3, body, 0)
        MIXC[s] = jnp.concatenate(
            [MIX[s * 3][:, 0:64], MIX[s * 3 + 1][:, 0:64], MIX[s * 3 + 2][:, 0:64]], axis=1
        ).astype(BF)

    def tb_desc(way, s, side, dist):
        heads = pl.ds(s * 3, 3)
        return copy(
            TBS.at[way, side, heads],
            TBR.at[way, side, dist - 1, heads],
            tb_s.at[way, s, side, dist - 1],
            tb_r.at[way, s, side, dist - 1],
            along(dist if side == 0 else 4 - dist),
        )

    def tb_each(act):
        for side in range(2):
            for dist in (1, 2):

                @pl.when(reaches(1 - side, dist))
                def _():
                    act(side, dist)

    def tb_send(way, s):
        tb_each(lambda side, dist: tb_desc(way, s, side, dist).start())

    def tb_take(way, s, comb):
        for side in range(2):
            for dist in (1, 2):

                @pl.when(reaches(side, dist))
                def _():
                    tb_desc(way, s, side, dist).wait_recv()

            both = (edge(s, side, 1) == edge(s, side, 2)) & reaches(side, 2)
            both = jnp.broadcast_to(both, (TAB, 256))
            for h in range(3):
                i = s * 3 + h
                near = TBR[way, side, 0, i].astype(F32)
                total = near + jnp.where(both, TBR[way, side, 1, i].astype(F32), 0.0)
                comb[i, 128 * side : 128 * side + TAB, :] = total.astype(BF)

    def attn_out(s):
        P[s] = nt(MIXC[s], WO[...])

    gain_attn, shift_attn, gain_ffn, shift_ffn, bias_down = (
        ref[...].reshape(1, 768) for ref in (ga_ref, sa_ref, gf_ref, sf_ref, bd_ref)
    )
    ARS[0] = jnp.zeros((8, 768), F32)

    def add_small(row, value):
        ARS[0, row : row + 1, :] = ARS[0, row : row + 1, :] + value

    def over_rows(value):
        return jnp.sum(value, 0, keepdims=True)

    def norm_one(s, attn):
        normed, inv_std = norm_stats(x_ref[s].astype(F32) + attn)
        first = normed * gain_attn + shift_attn
        NORM1[s], FIRST[s] = normed, first
        INV1[s] = jnp.broadcast_to(inv_std, (64, 128))
        FI[s, chunk(t), :] = first.astype(BF)

    def norm_two(s, branch):
        normed, inv_std = norm_stats(FIRST[s] + branch + bias_down)
        out_ref[s] = (normed * gain_ffn + shift_ffn).astype(BF)
        cot = cot_ref[s].astype(F32)
        grad = norm_grad(cot, normed, inv_std, gain_ffn)
        GH2[s] = grad
        G2[s, chunk(t), :] = grad.astype(BF)
        add_small(2, over_rows(cot * normed))
        add_small(3, over_rows(cot))
        add_small(4, over_rows(grad))

    def norm_one_back(s, summed):
        grad_first = GH2[s] + summed
        normed = NORM1[s]
        grad = norm_grad(grad_first, normed, INV1[s][:, 0:1], gain_attn)
        GH1[s] = grad
        G1[s, chunk(t), :] = grad.astype(BF)
        add_small(0, over_rows(grad_first * normed))
        add_small(1, over_rows(grad_first))

    def tile(j):
        return pl.ds(pl.multiple_of(j * 256, 256), 256)

    def ffn_up(s):
        def body(j, carry):
            upper = nn(FI[s], WU[:, tile(j)]) + bu_ref[tile(j)].reshape(1, 256)
            cdf = 0.5 * (1.0 + lax.erf(upper * root_half))
            HID[s, :, tile(j)] = (upper * cdf).astype(BF)
            SLOPE[s, :, tile(j)] = cdf + upper * inv_root_tau * jnp.exp(-0.5 * upper * upper)
            return carry

        lax.fori_loop(0, 3, body, 0)

    def ffn_down(s):
        def body(j, carry):
            P[s, :, tile(j)] = nt(HID[s], WD[tile(j), :])
            return carry

        lax.fori_loop(0, 3, body, 0)

    def ffn_back_hidden(s):
        def body(j, carry):
            grad = (nn(G2[s], WD[:, tile(j)]) * SLOPE[s, :, tile(j)]).astype(BF)
            GUP[s, :, tile(j)] = grad
            ARS[0, 5:6, tile(j)] = ARS[0, 5:6, tile(j)] + over_rows(grad.astype(F32))
            return carry

        lax.fori_loop(0, 3, body, 0)

    def ffn_back_rows(s):
        def body(j, carry):
            P[s, :, tile(j)] = nt(GUP[s], WU[tile(j), :])
            return carry

        lax.fori_loop(0, 3, body, 0)

    def slots(i):
        narrow, wide = (GON, YSN, YRN, ZSN, ZRN), (GOW, YSW, YRW, ZSW, ZRW)
        return [ref.at[i] for ref in narrow] if i < 4 else [ref.at[i - 4] for ref in wide]

    def half_lanes(yy, j):
        return pl.ds(pl.multiple_of(yy * 384 + j * 128, 128), 128)

    def weight_grad(i, left, right):
        own_half, sent = slots(i)[0], slots(i)[1]

        def made(yy, j):
            lanes = half_lanes(yy, j)
            return tn(left[0, :, lanes], right[0]) + tn(left[1, :, lanes], right[1])

        def rows(j):
            return pl.ds(pl.multiple_of(j * 128, 128), 128)

        def other(j, carry):
            sent[rows(j), :] = made(1 - y, j).astype(BF)
            return carry

        def here(j, carry):
            own_half[rows(j), :] = made(y, j)
            return carry

        lax.fori_loop(0, 3, other, 0)
        for n in range(4):
            block = (z + (2, 1, 3, 0)[n]) % 4 if i < 4 else n + (1 - z // 2) * (3 - 2 * n)
            gy_desc(i, block).start()
        lax.fori_loop(0, 3, here, 0)

    def z_rows(block):
        return pl.ds(pl.multiple_of(block * 96, 96), 96)

    def gy_desc(i, block):
        sent, came_y = slots(i)[1:3]
        return copy(sent.at[z_rows(block), :], came_y.at[block], gy_s.at[i, block], gy_r.at[i, block], yp)

    def gz_desc(i, d):
        sent, came_z = slots(i)[3:5]
        return copy(sent.at[d - 1], came_z.at[d - 1], gz_s.at[i, d - 1], gz_r.at[i, d - 1], along(d))

    def chip_sum(i, block):
        own_half, _, came_y, _, _ = slots(i)
        gy_desc(i, block).wait_recv()
        return own_half[z_rows(block), :] + came_y[block].astype(F32)

    def g_pass(i):
        sent = slots(i)[3]
        for d in (2, 1, 3):
            sent[d - 1] = chip_sum(i, (z + d) % 4).astype(BF)
            gz_desc(i, d).start()

    def gc_desc(i, way, e):
        sent, came_z = ZSW.at[i - 4, way, e], ZRW.at[i - 4, way, e]
        return copy(sent, came_z, gc_s.at[i - 4, way, e], gc_r.at[i - 4, way, e], along(4 + step_of(way)))

    def gives(way, e):
        return z + e < 3 if way == 0 else z > e

    def behind(way):
        return z > 0 if way == 0 else z < 3

    def g_relay(i, e):
        for way in range(2):

            @pl.when(gives(way, e))
            def _():
                total = chip_sum(i, (z + 4 + (e + 1) * step_of(way)) % 4)
                ZSW[i - 4, way, e] = total.astype(BF)
                if e < 2:

                    @pl.when(behind(way))
                    def _():
                        gc_desc(i, way, e + 1).wait_recv()
                        ZSW[i - 4, way, e] = (total + ZRW[i - 4, way, e + 1].astype(F32)).astype(BF)

                gc_desc(i, way, e).start()

    def g_last(i, out):
        total = chip_sum(i, z)
        if i < 4:
            arrived = slots(i)[4]
            for d in (1, 2, 3):
                gz_desc(i, d).wait_recv()
                total = total + arrived[d - 1].astype(F32)
            out[...] = total
            return
        out[...] = total
        for way in range(2):

            @pl.when(behind(way))
            def _():
                gc_desc(i, way, 0).wait_recv()
                out[...] = out[...] + ZRW[i - 4, way, 0].astype(F32)

    def ar_desc(stage):
        where = (sib, far, yp)[stage]
        return copy(ARS.at[stage], ARR.at[stage], ar_s.at[stage], ar_r.at[stage], where)

    def ar_take(stage):
        ar_desc(stage).wait_recv()
        came = ARR[stage]
        if stage < 2:
            rows = lax.broadcasted_iota(jnp.int32, (8, 768), 0)
            came = jnp.where(rows < 5, came, 0.0)
        ARS[stage + 1] = ARS[stage] + came

    def ar_z_desc(i):
        return copy(ARS.at[3], ARZ.at[z], ar_s.at[3 + i], ar_r.at[3 + i], along(1 + i))

    def ar_z_start():
        ARZ[z] = ARS[3]
        for i in range(3):
            ar_z_desc(i).start()

    def ar_z_take():
        for i in range(3):
            ar_z_desc(i).wait_recv()
        small_ref[...] = (ARZ[0] + ARZ[1]) + (ARZ[2] + ARZ[3])

    def grad_tables(s):
        GM[...] = nn(G1[s], WO[...])
        lane = lanes_of((256, 128))
        zero = jnp.zeros((256, 64), F32)
        for h in range(3):
            i = s * 3 + h
            gm = jnp.concatenate([GM[:, 64 * h : 64 * h + 64], zero], axis=1)
            denom = DEN[i]
            slope = -jnp.sum(gm * MIX[i], -1, keepdims=True) / denom
            s_hi = slope.astype(BF).astype(F32)
            ext = jnp.where(lane == 64, s_hi, gm / denom)
            GX[i] = jnp.where(lane == 65, slope - s_hi, ext).astype(BF)

        def body(h, carry):
            i = s * 3 + h
            made = tables(GX[i], PQ[i], s)
            TBS[1, 1, i] = made[0:TAB].astype(BF)
            TBS[1, 0, i] = made[TAB : 2 * TAB].astype(BF)
            return carry

        lax.fori_loop(0, 3, body, 0)

    def pair(ext, s):
        ext = ext.astype(F32)
        return jnp.concatenate([ext * CM[0, s], ext * CM[1, s]], axis=1).astype(BF)

    def through_phi(grad_phi, phi, scaled, h):
        both = nn((grad_phi * phi).astype(BF), OMT[h])
        both = both[:, 0:128] + both[:, 128:256]
        return (both - scaled * both[:, 64:65]) * HEAD_DIM ** (-0.25)

    def side_by_side(heads):
        return jnp.concatenate([heads[h][:, 0:64] for h in range(3)], axis=1).astype(BF)

    def back_queries(s):
        def body(h, carry):
            i = s * 3 + h
            ext = GX[i]
            pairs = jnp.where(MSK[s] > 0, nt(ext, VX[i]), 0.0).astype(BF)
            grad = nn(pairs, PK[i]) + nn(pair(ext, s), COMB[i])
            GM3[h] = through_phi(grad, PQF[i], RQ[i], h)
            GKL[i] = tn(pairs, PQ[i])
            GVL[i] = tn(SS[i], ext)
            return carry

        lax.fori_loop(0, 3, body, 0)
        RGQ[s] = side_by_side(GM3)

    def back_keys(s):
        tb_take(1, s, GCOMB)

        def body(h, carry):
            i = s * 3 + h
            grad = GKL[i] + nn(pair(VX[i], s), GCOMB[i])
            GM3[h] = through_phi(grad, PKF[i], RK[i], h)
            cross = nt(PK[i], GCOMB[i])
            gv = GVL[i] + jnp.where(CM[0, s] > 0, cross[:, 0:128], 0.0)
            GV3[h] = gv + jnp.where(CM[1, s] > 0, cross[:, 128:256], 0.0)
            return carry

        lax.fori_loop(0, 3, body, 0)
        RGK[s] = side_by_side(GM3)
        RGV[s] = side_by_side(GV3)

    def input_rows(s):
        def body(j, carry):
            made = nt(RGQ[s], WQ[tile(j), :]) + nt(RGK[s], WK[tile(j), :])
            P[s, :, tile(j)] = made + nt(RGV[s], WV[tile(j), :])
            return carry

        lax.fori_loop(0, 3, body, 0)

    w_send(3)
    w_send(4)
    w_pass(2)
    w_wait(0)
    w_wait(1)
    ag_wait(0, X, 0)
    project_keys(0)
    keys(0)
    tb_send(0, 0)
    w_relay(4, 0)
    w_pass(3)
    ag_wait(0, X, 1)
    project_keys(1)
    keys(1)
    tb_send(0, 1)
    w_relay(4, 1)
    w_wait(2)
    project_queries(0)
    queries(0)
    w_relay(4, 2)
    project_queries(1)
    queries(1)
    w_send(5)
    mixing(0)
    w_wait(3)
    attn_out(0)
    rs_start(0, 0)
    mixing(1)
    attn_out(1)
    rs_start(0, 1)
    rs_mid(0, 0)
    rs_mid(0, 1)
    w_relay(5, 0)
    norm_one(0, rs_fin(0, 0))
    ag_start(1, FI, 0)
    norm_one(1, rs_fin(0, 1))
    ag_start(1, FI, 1)
    w_relay(5, 1)
    ag_pass(1, FI, 0)
    ag_pass(1, FI, 1)
    w_relay(5, 2)
    ag_wait(1, FI, 0)
    w_wait(4)
    ffn_up(0)
    w_wait(5)
    ffn_down(0)
    rs_start(1, 0)
    ag_wait(1, FI, 1)
    ffn_up(1)
    rs_mid(1, 0)
    ffn_down(1)
    rs_start(1, 1)
    norm_two(0, rs_fin(1, 0))
    ag_start(2, G2, 0)
    rs_mid(1, 1)
    norm_two(1, rs_fin(1, 1))
    ag_start(2, G2, 1)
    ag_pass(2, G2, 0)
    ag_pass(2, G2, 1)
    ag_wait(2, G2, 0)
    ffn_back_hidden(0)
    ffn_back_rows(0)
    rs_start(2, 0)
    ag_wait(2, G2, 1)
    ffn_back_hidden(1)
    rs_mid(2, 0)
    ffn_back_rows(1)
    rs_start(2, 1)
    weight_grad(5, G2, HID)
    rs_mid(2, 1)
    norm_one_back(0, rs_fin(2, 0))
    ag_start(3, G1, 0)
    norm_one_back(1, rs_fin(2, 1))
    ag_start(3, G1, 1)
    ar_desc(0).start()
    weight_grad(4, FI, GUP)
    ag_pass(3, G1, 0)
    g_relay(5, 2)
    ag_pass(3, G1, 1)
    ar_take(0)
    ar_desc(1).start()
    ag_wait(3, G1, 0)
    grad_tables(0)
    tb_send(1, 0)
    ag_wait(3, G1, 1)
    grad_tables(1)
    tb_send(1, 1)
    weight_grad(3, G1, MIXC)
    g_relay(5, 1)
    ar_take(1)
    ar_desc(2).start()
    back_queries(0)
    g_relay(5, 0)
    back_queries(1)
    weight_grad(2, X, RGQ)
    g_relay(4, 2)
    ar_take(2)
    ar_z_start()
    back_keys(0)
    g_relay(4, 1)
    input_rows(0)
    rs_start(3, 0)
    back_keys(1)
    rs_mid(3, 0)
    weight_grad(0, X, RGK)
    weight_grad(1, X, RGV)
    g_relay(4, 0)
    input_rows(1)
    rs_start(3, 1)
    g_pass(3)
    g_pass(2)
    rs_mid(3, 1)
    g_pass(0)
    g_pass(1)
    gin_ref[0] = (GH1[0] + rs_fin(3, 0)).astype(BF)
    gin_ref[1] = (GH1[1] + rs_fin(3, 1)).astype(BF)
    ar_z_take()
    g_last(5, od_ref)
    g_last(4, ou_ref)
    g_last(3, oo_ref)
    g_last(2, oq_ref)
    g_last(0, ok_ref)
    g_last(1, ov_ref)

    for s in range(2):
        for op, buf in enumerate((X, FI, G2, G1)):
            for which in range(3):
                ag_desc(op, buf, s, which).wait_send()
        for op in range(4):
            sib_desc(op, s, 0).wait_send()
            sib_desc(op, s, 1).wait_send()
            xrs_desc(op, s).wait_send()
        for way in range(2):
            tb_each(lambda side, dist: tb_desc(way, s, side, dist).wait_send())
    for i in range(6):
        wy_desc(i, 0).wait_send()
        for block in range(4):
            gy_desc(i, block).wait_send()
        for d in (1, 2, 3):
            if i < 4:
                wy_desc(i, d).wait_send()
                wz_desc(i, d).wait_send()
                gz_desc(i, d).wait_send()
    for i in (4, 5):
        for way in range(2):
            for j in range(3):

                @pl.when(goes(way, j))
                def _():
                    wc_desc(i, way, j).wait_send()

                @pl.when(came(way, j))
                def _():
                    wf_desc(i, way, j).wait_send()

                @pl.when(gives(way, j))
                def _():
                    gc_desc(i, way, j).wait_send()

    for stage in range(3):
        ar_desc(stage).wait_send()
        ar_z_desc(stage).wait_send()
        seg_desc(stage + 1).wait_send()


def hand_out(
    out_ref, gin_ref, ok_ref, ov_ref, oq_ref, oo_ref, ou_ref, od_ref, small_ref,
    out_o, gin_o, q_o, k_o, v_o, o_o, ga_o, sa_o, u_o, bu_o, d_o, bd_o, gf_o, sf_o,
):
    pairs = ((out_o, out_ref), (gin_o, gin_ref), (q_o, oq_ref), (k_o, ok_ref), (v_o, ov_ref), (u_o, ou_ref))
    for dst, src in pairs:
        dst[...] = src[...]
    o_o[...] = oo_ref[...].T
    d_o[...] = od_ref[...].T
    for row, dst in enumerate((ga_o, sa_o, gf_o, sf_o, bd_o, bu_o)):
        dst[...] = small_ref[row, :]


def dma(*shape):
    return pltpu.SemaphoreType.DMA(shape)


def fast_device(
    inputs, seg_ids, feature_map, w_query, w_key, w_value, w_out, gain_attn, shift_attn,
    w_up, bias_up, w_down, bias_down, gain_ffn, shift_ffn, cotangent,
):
    vm = pltpu.VMEM
    scratch = [
        vm((2, 256, 768), BF), vm((2, 256, 768), BF), vm((2, 256, 768), BF), vm((2, 256, 768), BF),
        vm((768, 192), BF), vm((768, 192), BF), vm((768, 192), BF), vm((768, 192), BF),
        vm((768, 768), BF), vm((768, 768), BF), vm((96, 192), BF), vm((96, 768), BF),
        vm((2, 256, 768), F32), vm((2, 256, 768), BF), vm((2, 256, 768), F32), vm((2, 256, 768), BF),
        vm((2, 64, 768), F32), vm((2, 64, 768), F32), vm((2, 64, 128), F32),
        vm((2, 64, 768), F32), vm((2, 64, 768), F32),
        vm((6, 256, 128), F32), vm((6, 256, 128), F32), vm((6, 256, 128), BF),
        vm((6, 256, 256), F32), vm((6, 256, 256), F32), vm((6, 256, 256), BF), vm((6, 256, 256), BF),
        vm((6, 256, 256), BF),
        vm((2, 256, 256), F32), vm((2, 2, 256, 128), F32), vm((4, 2, 256), jnp.int32),
        vm((3, 256, 256), BF), vm((3, 128, 256), BF), vm((3, 256, 256), BF),
        vm((6, 256, 128), F32), vm((6, 256, 128), F32), vm((6, 256, 128), BF),
        vm((6, 256, 256), F32), vm((6, 256, 128), F32),
        vm((256, 192), F32), vm((3, 256, 128), F32), vm((3, 256, 128), F32),
        vm((2, 256, 192), BF), vm((2, 256, 192), BF), vm((2, 256, 192), BF), vm((2, 256, 192), BF),
        vm((2, 2, 6, TAB, 256), BF), vm((2, 2, 2, 6, TAB, 256), BF), vm((6, 256, 256), BF), vm((6, 256, 256), BF),
        vm((4, 2, 2, 64, 768), BF), vm((4, 2, 2, 64, 768), BF), vm((4, 2, 64, 768), BF), vm((4, 2, 64, 768), BF),
        vm((4, 384, 192), F32), vm((2, 384, 768), F32),
        vm((4, 384, 192), BF), vm((2, 384, 768), BF),
        vm((4, 4, 96, 192), BF), vm((2, 4, 96, 768), BF),
        vm((4, 3, 96, 192), BF), vm((2, 2, 3, 96, 768), BF),
        vm((4, 3, 96, 192), BF), vm((2, 2, 3, 96, 768), BF),
        vm((4, 8, 768), F32), vm((3, 8, 768), F32), vm((4, 8, 768), F32),
        dma(4, 2, 3), dma(4, 2, 3), dma(4, 2, 3), dma(4, 2, 3), dma(3), dma(3),
        dma(4, 3), dma(4, 3), dma(6, 4), dma(6, 4), dma(2, 2, 3), dma(2, 2, 3), dma(2, 2, 3), dma(2, 2, 3),
        dma(6, 4), dma(6, 4), dma(4, 3), dma(4, 3), dma(2, 2, 3), dma(2, 2, 3),
        dma(2, 2, 2, 2), dma(2, 2, 2, 2), dma(6), dma(6),
    ]
    in_vmem = pl.BlockSpec(memory_space=pltpu.VMEM)
    shape = jax.ShapeDtypeStruct
    narrow, wide, rows, vec = shape((96, 192), F32), shape((96, 768), F32), shape((2, 64, 768), BF), shape((768,), F32)
    made = pl.pallas_call(
        layer_kernel,
        out_shape=(rows, rows, narrow, narrow, narrow, narrow, wide, wide, shape((8, 768), F32)),
        in_specs=[in_vmem] * 16,
        out_specs=(in_vmem,) * 9,
        scratch_shapes=scratch,
        compiler_params=pltpu.CompilerParams(
            collective_id=0, has_side_effects=True, vmem_limit_bytes=67043328
        ),
    )(
        inputs, seg_ids, feature_map, w_query, w_key, w_value, w_out, gain_attn, shift_attn,
        w_up, bias_up, w_down, bias_down, gain_ffn, shift_ffn, cotangent,
    )
    return pl.pallas_call(
        hand_out,
        out_shape=(
            rows, rows, narrow, narrow, narrow, shape((192, 96), F32), vec, vec,
            wide, vec, shape((768, 96), F32), vec, vec, vec,
        ),
        in_specs=[in_vmem] * 9,
        out_specs=(in_vmem,) * 14,
    )(*made)


def solution(mesh):
    placed = (
        P("shard", ("ctx", "tp"), None),
        P("shard", "ctx"),
        P("tp", None, None),
        P(("shard", "ctx"), "tp"),
        P(("shard", "ctx"), "tp"),
        P(("shard", "ctx"), "tp"),
        P("tp", ("shard", "ctx")),
        P(),
        P(),
        P(("shard", "ctx"), "tp"),
        P("tp"),
        P("tp", ("shard", "ctx")),
        P(),
        P(),
        P(),
        P("shard", ("ctx", "tp"), None),
    )
    sizes = tuple(mesh.shape[axis] for axis in ("shard", "ctx", "tp"))
    return jax.shard_map(
        fast_device if sizes == (2, 4, 4) else per_device,
        mesh=mesh,
        in_specs=placed,
        out_specs=(
            P("shard", ("ctx", "tp"), None),
            P("shard", ("ctx", "tp"), None),
            P(("shard", "ctx"), "tp"),
            P(("shard", "ctx"), "tp"),
            P(("shard", "ctx"), "tp"),
            P("tp", ("shard", "ctx")),
            P(),
            P(),
            P(("shard", "ctx"), "tp"),
            P("tp"),
            P("tp", ("shard", "ctx")),
            P(),
            P(),
            P(),
        ),
        check_vma=False,
    )
```

```python
import jax
import jax.numpy as jnp
from jax import lax
from jax.experimental import pallas as pl
from jax.experimental.pallas import tpu as pltpu
from jax.sharding import PartitionSpec as P

HEAD_DIM = 64
FEATS = 256
FF = 3072
SEGS = 8


highest = lax.Precision.HIGHEST
root_half = 0.7071067811865476
inv_root_tau = 0.3989422804014327
norm_eps = 1e-05


def gelu_value(upper):
    return upper * 0.5 * (1.0 + lax.erf(upper * root_half))


def gelu_slope(upper):
    return 0.5 * (1.0 + lax.erf(upper * root_half)) + upper * inv_root_tau * jnp.exp(
        -0.5 * upper * upper
    )


def layer_norm(hidden_in, gain_vec, shift_vec):
    mean_val = jnp.mean(hidden_in, -1, keepdims=True)
    centred = hidden_in - mean_val
    inv_std = lax.rsqrt(jnp.mean(centred * centred, -1, keepdims=True) + norm_eps)
    normed = centred * inv_std
    return (normed * gain_vec + shift_vec, normed, inv_std)


def norm_back(grad_in, normed, inv_std, gain_vec):
    scaled = grad_in * gain_vec
    grad_hidden = inv_std * (
        scaled
        - jnp.mean(scaled, -1, keepdims=True)
        - normed * jnp.mean(scaled * normed, -1, keepdims=True)
    )
    return (grad_hidden, jnp.sum(grad_in * normed, (0, 1)), jnp.sum(grad_in, (0, 1)))


def features(projected, omega_local):
    seq_count, ctx_rows, width = projected.shape
    heads_here = omega_local.shape[0]
    scaled = projected.reshape(seq_count, ctx_rows, heads_here, HEAD_DIM) * HEAD_DIM ** (-0.25)
    angles = jnp.einsum("schd,hdm->schm", scaled, omega_local, precision=highest)
    squares = 0.5 * jnp.sum(scaled * scaled, -1, keepdims=True)
    return (jnp.exp(angles - squares) * FEATS ** (-0.5), scaled)


def feature_back(grad_phi, phi_full, scaled, omega_local):
    grad_angle = grad_phi * phi_full
    grad_scaled = jnp.einsum("schm,hdm->schd", grad_angle, omega_local, precision=highest)
    grad_scaled = grad_scaled - scaled * jnp.sum(grad_angle, -1, keepdims=True)
    seq_count, ctx_rows, heads_here, head_width = scaled.shape
    return (grad_scaled * HEAD_DIM ** (-0.25)).reshape(seq_count, ctx_rows, heads_here * head_width)


def spread_rows(mask_low, left):
    ctx_rows, heads_here, feat_count = left.shape
    wide = mask_low[:, None, :, None] * left[:, :, None, :]
    return wide.reshape(ctx_rows, heads_here, -1)


def segment_outer(operands):
    mask_low, left, right = operands
    return jnp.einsum(
        "chx,che->hxe", spread_rows(mask_low, left), right, preferred_element_type=jnp.float32
    )


def segment_apply(operands):
    mask_low, left, table = operands
    return jnp.einsum(
        "chx,hxe->che", spread_rows(mask_low, left), table, preferred_element_type=jnp.float32
    )


def segment_back(operands):
    mask_full, left, table = operands
    ctx_rows, heads_here, width = left.shape
    seg_count = mask_full.shape[1]
    wide = jnp.einsum("che,hxe->chx", left, table, preferred_element_type=jnp.float32)
    wide = wide.reshape(ctx_rows, heads_here, seg_count, -1)
    return jnp.sum(wide * mask_full[:, None, :, None], 2)


def inner_product(left, right):
    return lax.dot_general(
        left, right, (((0,), (0,)), ((), ())), preferred_element_type=jnp.float32
    )


def right_transposed(left, right):
    return lax.dot_general(
        left, right, (((1,), (1,)), ((), ())), preferred_element_type=jnp.float32
    )


def per_device(
    inputs,
    seg_ids,
    feature_map,
    w_query,
    w_key,
    w_value,
    w_out,
    gain_attn,
    shift_attn,
    w_up,
    bias_up,
    w_down,
    bias_down,
    gain_ffn,
    shift_ffn,
    cotangent,
):
    full_query, full_key, full_value, full_up, full_out, full_down = (
        lax.all_gather(w_query, ("shard", "ctx"), axis=0, tiled=True),
        lax.all_gather(w_key, ("shard", "ctx"), axis=0, tiled=True),
        lax.all_gather(w_value, ("shard", "ctx"), axis=0, tiled=True),
        lax.all_gather(w_up, ("shard", "ctx"), axis=0, tiled=True),
        lax.all_gather(w_out, ("shard", "ctx"), axis=1, tiled=True),
        lax.all_gather(w_down, ("shard", "ctx"), axis=1, tiled=True),
    )
    seq_count, row_share, width = inputs.shape
    rows_all = lax.all_gather(inputs, "tp", axis=1, tiled=True)
    ctx_rows = rows_all.shape[1]
    token_count = seq_count * ctx_rows
    flat = rows_all.reshape(token_count, width)
    heads_here = feature_map.shape[0]
    head_cols = heads_here * HEAD_DIM
    query_proj = jnp.dot(flat, full_query, preferred_element_type=jnp.float32).reshape(
        seq_count, ctx_rows, head_cols
    )
    key_proj = jnp.dot(flat, full_key, preferred_element_type=jnp.float32).reshape(
        seq_count, ctx_rows, head_cols
    )
    value_low = jnp.dot(flat, full_value, preferred_element_type=jnp.float32).astype(jnp.bfloat16)
    value_low = value_low.reshape(seq_count, ctx_rows, head_cols)
    value_four = value_low.reshape(seq_count, ctx_rows, heads_here, HEAD_DIM)
    phi_query, scaled_query = features(query_proj, feature_map)
    phi_key, scaled_key = features(key_proj, feature_map)
    phq_low = phi_query.astype(jnp.bfloat16)
    phk_low = phi_key.astype(jnp.bfloat16)
    matches = seg_ids[:, :, None] == jnp.arange(SEGS, dtype=jnp.int32)[None, None, :]
    mask_low = matches.astype(jnp.bfloat16)
    mask_full = matches.astype(jnp.float32)
    kv_part = lax.map(segment_outer, (mask_low, phk_low, value_four))
    z_part = jnp.einsum("scg,schm->shgm", mask_low, phk_low, preferred_element_type=jnp.float32)
    kv_sum, z_sum = lax.psum((kv_part, z_part), "ctx")
    kv_low = kv_sum.astype(jnp.bfloat16)
    numer = lax.map(segment_apply, (mask_low, phq_low, kv_low))
    phq_wide = phq_low.astype(jnp.float32)
    denom = jnp.sum(
        jnp.einsum("schm,shgm->schg", phq_wide, z_sum, precision=highest)
        * mask_full[:, :, None, :],
        -1,
    )
    mixed = numer / denom[..., None]
    mixed_low = mixed.astype(jnp.bfloat16).reshape(seq_count, ctx_rows, head_cols)
    piece = mixed_low
    attn_sum = jnp.swapaxes(
        lax.psum_scatter(
            jnp.einsum("scf,fd->csd", piece, full_out, preferred_element_type=jnp.float32),
            "tp",
            scatter_dimension=0,
            tiled=True,
        ),
        0,
        1,
    )
    first, normed_one, inv_one = layer_norm(
        inputs.astype(jnp.float32) + attn_sum, gain_attn, shift_attn
    )
    first_low = first.astype(jnp.bfloat16)
    first_rows = lax.all_gather(first_low, "tp", axis=1, tiled=True)
    first_flat = first_rows.reshape(token_count, width)
    upper = jnp.dot(first_flat, full_up, preferred_element_type=jnp.float32) + bias_up
    ffn_here = upper.shape[1]
    hidden_low = gelu_value(upper).astype(jnp.bfloat16)
    hidden_three = hidden_low.reshape(seq_count, ctx_rows, ffn_here)
    piece = hidden_three
    branch = jnp.swapaxes(
        lax.psum_scatter(
            jnp.einsum("scf,fd->csd", piece, full_down, preferred_element_type=jnp.float32),
            "tp",
            scatter_dimension=0,
            tiled=True,
        ),
        0,
        1,
    )
    final, normed_two, inv_two = layer_norm(first + branch + bias_down, gain_ffn, shift_ffn)
    outputs = final.astype(jnp.bfloat16)
    full_query, full_key, full_value, full_up, full_out, full_down = (
        lax.all_gather(w_query, ("shard", "ctx"), axis=0, tiled=True),
        lax.all_gather(w_key, ("shard", "ctx"), axis=0, tiled=True),
        lax.all_gather(w_value, ("shard", "ctx"), axis=0, tiled=True),
        lax.all_gather(w_up, ("shard", "ctx"), axis=0, tiled=True),
        lax.all_gather(w_out, ("shard", "ctx"), axis=1, tiled=True),
        lax.all_gather(w_down, ("shard", "ctx"), axis=1, tiled=True),
    )
    grad_final = cotangent.astype(jnp.float32)
    grad_two, grad_gain_ffn, grad_shift_ffn = norm_back(grad_final, normed_two, inv_two, gain_ffn)
    grad_bias_down = jnp.sum(grad_two, (0, 1))
    grad_two_rows = lax.all_gather(grad_two.astype(jnp.bfloat16), "tp", axis=1, tiled=True)
    grad_two_flat = grad_two_rows.reshape(token_count, width)
    grad_hidden = right_transposed(grad_two_flat, full_down)
    grad_upper = (grad_hidden * gelu_slope(upper)).astype(jnp.bfloat16)
    grad_down = inner_product(hidden_low, grad_two_flat)
    grad_up = inner_product(first_flat, grad_upper)
    grad_bias_local = jnp.sum(grad_upper.astype(jnp.float32), 0)
    grad_upper_three = grad_upper.reshape(seq_count, ctx_rows, ffn_here)
    piece = grad_upper_three
    grad_first = grad_two + jnp.swapaxes(
        lax.psum_scatter(
            jnp.einsum("scf,df->csd", piece, full_up, preferred_element_type=jnp.float32),
            "tp",
            scatter_dimension=0,
            tiled=True,
        ),
        0,
        1,
    )
    grad_one, grad_gain_attn, grad_shift_attn = norm_back(
        grad_first, normed_one, inv_one, gain_attn
    )
    grad_one_rows = lax.all_gather(grad_one.astype(jnp.bfloat16), "tp", axis=1, tiled=True)
    grad_one_flat = grad_one_rows.reshape(token_count, width)
    grad_out = inner_product(mixed_low.reshape(token_count, head_cols), grad_one_flat)
    grad_mixed = right_transposed(grad_one_flat, full_out).reshape(
        seq_count, ctx_rows, heads_here, HEAD_DIM
    )
    grad_numer = (grad_mixed / denom[..., None]).astype(jnp.bfloat16)
    grad_denom = -jnp.sum(grad_mixed * mixed, -1) / denom
    kv_grad_part = lax.map(segment_outer, (mask_low, phq_low, grad_numer))
    z_grad_part = jnp.einsum(
        "scg,schm->shgm", mask_full, phq_wide * grad_denom[..., None], precision=highest
    )
    kv_grad, z_grad = (
        lax.psum(kv_grad_part.astype(jnp.bfloat16), "ctx").astype(jnp.float32),
        lax.psum(z_grad_part.astype(jnp.bfloat16), "ctx").astype(jnp.float32),
    )
    kv_grad_low = kv_grad.astype(jnp.bfloat16)
    grad_phq = lax.map(segment_back, (mask_full, grad_numer, kv_low))
    grad_phq = grad_phq + grad_denom[..., None] * jnp.einsum(
        "scg,shgm->schm", mask_full, z_sum, precision=highest
    )
    grad_phk = lax.map(segment_back, (mask_full, value_four, kv_grad_low))
    grad_phk = grad_phk + jnp.einsum("scg,shgm->schm", mask_full, z_grad, precision=highest)
    grad_value_rows = lax.map(segment_apply, (mask_low, phk_low, kv_grad_low)).astype(jnp.bfloat16)
    grad_value_rows = grad_value_rows.reshape(seq_count, ctx_rows, head_cols)
    grad_query_rows = feature_back(grad_phq, phi_query, scaled_query, feature_map).astype(
        jnp.bfloat16
    )
    grad_key_rows = feature_back(grad_phk, phi_key, scaled_key, feature_map).astype(jnp.bfloat16)
    grad_query = inner_product(flat, grad_query_rows.reshape(token_count, head_cols))
    grad_key = inner_product(flat, grad_key_rows.reshape(token_count, head_cols))
    grad_value = inner_product(flat, grad_value_rows.reshape(token_count, head_cols))
    total = jnp.einsum(
        "scf,df->csd", grad_query_rows, full_query, preferred_element_type=jnp.float32
    )
    total = total + jnp.einsum(
        "scf,df->csd", grad_key_rows, full_key, preferred_element_type=jnp.float32
    )
    grad_rows = jnp.swapaxes(
        lax.psum_scatter(
            (
                total
                + jnp.einsum(
                    "scf,df->csd", grad_value_rows, full_value, preferred_element_type=jnp.float32
                )
            ).astype(jnp.bfloat16),
            "tp",
            scatter_dimension=0,
            tiled=True,
        ).astype(jnp.float32),
        0,
        1,
    )
    grad_inputs = (grad_one + grad_rows).astype(jnp.bfloat16)
    grad_query, grad_key, grad_value, grad_up, grad_out, grad_down = (
        lax.psum_scatter(grad_query, ("shard", "ctx"), scatter_dimension=0, tiled=True),
        lax.psum_scatter(grad_key, ("shard", "ctx"), scatter_dimension=0, tiled=True),
        lax.psum_scatter(grad_value, ("shard", "ctx"), scatter_dimension=0, tiled=True),
        lax.psum_scatter(grad_up, ("shard", "ctx"), scatter_dimension=0, tiled=True),
        lax.psum_scatter(grad_out, ("shard", "ctx"), scatter_dimension=1, tiled=True),
        lax.psum_scatter(grad_down, ("shard", "ctx"), scatter_dimension=1, tiled=True),
    )
    tp_index = lax.axis_index("tp")
    padded_bias = lax.dynamic_update_slice(
        jnp.zeros((FF,), jnp.float32), grad_bias_local, (tp_index * ffn_here,)
    )
    grad_gain_attn, grad_shift_attn, grad_gain_ffn, grad_shift_ffn, grad_bias_down, padded_bias = (
        lax.psum(
            (
                grad_gain_attn,
                grad_shift_attn,
                grad_gain_ffn,
                grad_shift_ffn,
                grad_bias_down,
                padded_bias,
            ),
            ("shard", "ctx", "tp"),
        )
    )
    grad_bias_up = lax.dynamic_slice(padded_bias, (tp_index * ffn_here,), (ffn_here,))
    return (
        outputs,
        grad_inputs,
        grad_query,
        grad_key,
        grad_value,
        grad_out,
        grad_gain_attn,
        grad_shift_attn,
        grad_up,
        grad_bias_up,
        grad_down,
        grad_bias_down,
        grad_gain_ffn,
        grad_shift_ffn,
    )


BF = jnp.bfloat16
F32 = jnp.float32
MESH_ID = pl.DeviceIdType.MESH
TAB = 80
SUBS = 3


def nn(left, right):
    return lax.dot_general(left, right, (((1,), (0,)), ((), ())), preferred_element_type=F32)


def nt(left, right):
    return lax.dot_general(left, right, (((1,), (1,)), ((), ())), preferred_element_type=F32)


def tn(left, right):
    return lax.dot_general(left, right, (((0,), (0,)), ((), ())), preferred_element_type=F32)


def lanes_of(shape):
    return lax.broadcasted_iota(jnp.int32, shape, 1)


def norm_stats(hidden_in):
    centred = hidden_in - jnp.mean(hidden_in, -1, keepdims=True)
    inv_std = lax.rsqrt(jnp.mean(centred * centred, -1, keepdims=True) + norm_eps)
    return centred * inv_std, inv_std


def norm_grad(grad_in, normed, inv_std, gain_vec):
    scaled = grad_in * gain_vec
    return inv_std * (
        scaled
        - jnp.mean(scaled, -1, keepdims=True)
        - normed * jnp.mean(scaled * normed, -1, keepdims=True)
    )


def layer_kernel(
    x_ref, seg_ref, om_ref, wq_ref, wk_ref, wv_ref, wo_ref, ga_ref, sa_ref, wu_ref, bu_ref, wd_ref,
    bd_ref, gf_ref, sf_ref, cot_ref,
    out_ref, gin_ref, ok_ref, ov_ref, oq_ref, oo_ref, ou_ref, od_ref, small_ref,
    X, FI, G2, G1, WK, WV, WQ, WO, WU, WD, OWN_O, P, HID, SLOPE, GUP,
    FIRST, NORM1, INV1, GH2, GH1,
    RQ, RK, VX, PQF, PKF, PQ, PK, SS, MSK, CM, SEGZ,
    OM1, OM2, OMT,
    MIX, DEN, GX, GKL, GVL, GM, GM3, GV3, RGK, RGV, RGQ, MIXC,
    TBS, TBR, COMB, GCOMB,
    SIBS, SIBR, XS, XR,
    GON, GOW, YSN, YSW, YRN, YRW, ZSN, ZSW, ZRN, ZRW,
    ARS, ARR, ARZ,
    ag_s, ag_r, ra_s, ra_r, seg_s, seg_r, wz_s, wz_r, wy_s, wy_r, wc_s, wc_r, wf_s, wf_r, gy_s, gy_r, gz_s, gz_r, gc_s, gc_r, tb_s, tb_r, ar_s, ar_r,
):
    y = lax.axis_index("shard")
    z = lax.axis_index("ctx")
    t = lax.axis_index("tp")
    sib_t, far_t = t + 1 - 2 * (t % 2), 3 - t
    sib = {"tp": sib_t}
    far = {"tp": far_t}
    yp = {"shard": 1 - y}

    def along(d):
        return {"ctx": (z + d) % 4}

    def block_rows(yy, zz):
        return pl.ds(pl.multiple_of((yy * 4 + zz) * 96, 96), 96)

    def copy(src, dst, send, recv, where):
        return pltpu.make_async_remote_copy(
            src_ref=src, dst_ref=dst, send_sem=send, recv_sem=recv, device_id=where,
            device_id_type=MESH_ID,
        )

    barrier = pltpu.get_barrier_semaphore()
    for where in (sib, far, yp, along(1), along(2), along(3)):
        pl.semaphore_signal(barrier, inc=1, device_id=where, device_id_type=MESH_ID)
    pl.semaphore_wait(barrier, 6)

    def chunk(tt):
        return pl.ds(pl.multiple_of(tt * 64, 64), 64)

    def ag_desc(op, buf, s, which):
        rows = chunk(far_t) if which == 2 else chunk(t)
        where = far if which == 1 else sib
        return copy(
            buf.at[s, rows, :], buf.at[s, rows, :], ag_s.at[op, s, which], ag_r.at[op, s, which], where
        )

    def ag_start(op, buf, s):
        ag_desc(op, buf, s, 1).start()
        ag_desc(op, buf, s, 0).start()

    def ag_pass(op, buf, s):
        ag_desc(op, buf, s, 1).wait_recv()
        ag_desc(op, buf, s, 2).start()

    def ag_wait(op, buf, s):
        ag_desc(op, buf, s, 0).wait_recv()
        ag_desc(op, buf, s, 2).wait_recv()

    def sib_desc(op, s, part):
        return copy(
            SIBS.at[op, s, part], SIBR.at[op, s, part], ra_s.at[op, s, part], ra_r.at[op, s, part], sib
        )

    def xrs_desc(op, s):
        return copy(XS.at[op, s], XR.at[op, s], ra_s.at[op, s, 2], ra_r.at[op, s, 2], far)

    def part_rows(s, tt):
        return P[s, chunk(tt), :]

    def rs_start(op, s):
        SIBS[op, s, 0] = part_rows(s, (t + 2) % 4).astype(BF)
        sib_desc(op, s, 0).start()
        SIBS[op, s, 1] = part_rows(s, sib_t).astype(BF)
        sib_desc(op, s, 1).start()

    def rs_mid(op, s):
        sib_desc(op, s, 0).wait_recv()
        XS[op, s] = (part_rows(s, far_t) + SIBR[op, s, 0].astype(F32)).astype(BF)
        xrs_desc(op, s).start()

    def rs_fin(op, s):
        sib_desc(op, s, 1).wait_recv()
        kept = part_rows(s, t) + SIBR[op, s, 1].astype(F32)
        xrs_desc(op, s).wait_recv()
        return kept + XR[op, s].astype(F32)

    gathered = (WK, WV, WQ, WO, WU, WD)
    mine = (wk_ref, wv_ref, wq_ref, OWN_O, wu_ref, wd_ref)

    def wz_desc(i, d):
        dst = gathered[i].at[block_rows(y, z), :]
        return copy(mine[i], dst, wz_s.at[i, d - 1], wz_r.at[i, d - 1], along(d))

    def wy_desc(i, d):
        dst = gathered[i].at[block_rows(y, (z + 4 - d) % 4), :]
        return copy(mine[i] if d == 0 else dst, dst, wy_s.at[i, d], wy_r.at[i, d], yp)

    def step_of(way):
        return 1 - 2 * way

    def came(way, j):
        return z > j if way == 0 else z + j < 3

    def goes(way, j):
        return (z >= j) & (z < 3) if way == 0 else (z + j <= 3) & (z > 0)

    def wc_desc(i, way, j):
        dst = gathered[i].at[block_rows(y, (z + 4 - j * step_of(way)) % 4), :]
        src = mine[i] if j == 0 else dst
        return copy(src, dst, wc_s.at[i - 4, way, j], wc_r.at[i - 4, way, j], along(4 + step_of(way)))

    def wf_desc(i, way, j):
        part = gathered[i].at[block_rows(y, (z + 4 - (j + 1) * step_of(way)) % 4), :]
        return copy(part, part, wf_s.at[i - 4, way, j], wf_r.at[i - 4, way, j], yp)

    def w_send(i):
        if i < 4:
            for d in (2, 1, 3):
                wz_desc(i, d).start()
        else:
            for way in range(2):

                @pl.when(goes(way, 0))
                def _():
                    wc_desc(i, way, 0).start()

    def w_over(i):
        wy_desc(i, 0).start()

    def w_pass(i):
        for d in (2, 1, 3):
            wz_desc(i, d).wait_recv()
            wy_desc(i, d).start()

    def w_relay(i, j):
        for way in range(2):

            @pl.when(came(way, j))
            def _():
                wc_desc(i, way, j).wait_recv()

            if j < 2:

                @pl.when(goes(way, j + 1))
                def _():
                    wc_desc(i, way, j + 1).start()

            @pl.when(came(way, j))
            def _():
                wf_desc(i, way, j).start()

    def w_wait(i):
        wy_desc(i, 0).wait_recv()
        if i < 4:
            for d in (1, 2, 3):
                wy_desc(i, d).wait_recv()
            return
        for way in range(2):
            for j in range(3):

                @pl.when(came(way, j))
                def _():
                    wf_desc(i, way, j).wait_recv()

    for i in range(2):
        w_send(i)
        w_over(i)
    own = block_rows(y, z)
    for s in range(2):
        X[s, chunk(t), :] = x_ref[s]
        ag_start(0, X, s)
    w_send(2)
    w_over(2)
    TBR[...] = jnp.zeros_like(TBR)
    COMB[...] = jnp.zeros_like(COMB)
    GCOMB[...] = jnp.zeros_like(GCOMB)

    def seg_desc(d):
        return copy(seg_ref, SEGZ.at[z], seg_s.at[d - 1], seg_r.at[d - 1], along(d))

    for d in (1, 2, 3):
        seg_desc(d).start()
    WK[own, :] = wk_ref[...]
    WV[own, :] = wv_ref[...]
    WQ[own, :] = wq_ref[...]
    WU[own, :] = wu_ref[...]
    turned = wo_ref[...].T
    OWN_O[...] = turned
    WO[own, :] = turned
    WD[own, :] = wd_ref[...]

    def split_omega(h, carry):
        om = om_ref[h]
        hi = om.astype(BF)
        low = (om - hi.astype(F32)).astype(BF)
        zero = jnp.zeros((64, 256), BF)
        OM1[h] = jnp.concatenate([hi, zero, hi, zero], axis=0)
        OM2[h] = jnp.concatenate([low, zero], axis=0)
        turned = jnp.concatenate([om, jnp.zeros((64, 256), F32)], axis=0).T
        t_hi = turned.astype(BF)
        t_low = (turned - t_hi.astype(F32)).astype(BF)
        one_at = (lanes_of((256, 128)) == 64).astype(BF)
        OMT[h] = jnp.concatenate([t_hi + one_at, t_low], axis=1)
        return carry

    lax.fori_loop(0, 3, split_omega, 0)

    for s in range(2):
        ag_pass(0, X, s)
    w_pass(0)
    w_pass(1)

    for d in (1, 2, 3):
        seg_desc(d).wait_recv()
    seg_row = [seg_ref[s : s + 1, :] for s in range(2)]

    def edge(s, side, dist):
        if side == 0:
            return SEGZ[(z + 4 - dist) % 4, s : s + 1, 255:256]
        return SEGZ[(z + dist) % 4, s : s + 1, 0:1]

    def reaches(side, dist):
        return z >= dist if side == 0 else z + dist <= 3

    for s in range(2):
        wide = jnp.broadcast_to(seg_row[s].astype(F32), (256, 256))
        col = wide.T
        MSK[s] = (wide == col).astype(F32)
        for side in range(2):
            near = (col[:, 0:128] == edge(s, side, 1).astype(F32)).astype(F32)
            CM[side, s] = jnp.where(reaches(side, 1), near, 0.0)

    def first_row(s):
        return (seg_row[s] == seg_row[s][:, 0:1]).astype(F32)

    def last_row(s):
        return (seg_row[s] == seg_row[s][:, 255:256]).astype(F32)

    def project_keys(s):
        rows = X[s]
        made_k = nn(rows, WK[...]) * HEAD_DIM ** (-0.25)
        made_v = nn(rows, WV[...])
        zero = jnp.zeros((256, 64), F32)
        lane = lanes_of((256, 128))
        for h in range(3):
            i = s * 3 + h
            RK[i] = jnp.concatenate([made_k[:, 64 * h : 64 * h + 64], zero], axis=1)
            v_h = jnp.concatenate([made_v[:, 64 * h : 64 * h + 64], zero], axis=1)
            VX[i] = jnp.where((lane == 64) | (lane == 65), 1.0, v_h).astype(BF)

    def project_queries(s):
        made_q = nn(X[s], WQ[...]) * HEAD_DIM ** (-0.25)
        zero = jnp.zeros((256, 64), F32)
        for h in range(3):
            RQ[s * 3 + h] = jnp.concatenate([made_q[:, 64 * h : 64 * h + 64], zero], axis=1)

    def phi_of(scaled, h):
        hi = scaled.astype(BF)
        low = (scaled - hi.astype(F32)).astype(BF)
        angles = nn(jnp.concatenate([hi, low], axis=1), OM1[h]) + nn(hi, OM2[h])
        squares = 0.5 * jnp.sum(scaled * scaled, -1, keepdims=True)
        return jnp.exp(angles - squares) * FEATS ** (-0.5)

    def tables(ext, feats, s):
        turned = ext.astype(F32).T[0:TAB, :]
        both = jnp.concatenate([turned * first_row(s), turned * last_row(s)], axis=0)
        return nn(both.astype(BF), feats)

    def keys(s):
        def body(h, carry):
            i = s * 3 + h
            phi = phi_of(RK[i], h)
            PKF[i] = phi
            low = phi.astype(BF)
            PK[i] = low
            made = tables(VX[i], low, s)
            TBS[0, 1, i] = made[0:TAB].astype(BF)
            TBS[0, 0, i] = made[TAB : 2 * TAB].astype(BF)
            return carry

        lax.fori_loop(0, 3, body, 0, unroll=True)

    def queries(s):
        def body(h, carry):
            i = s * 3 + h
            phi = phi_of(RQ[i], h)
            PQF[i] = phi
            low = phi.astype(BF)
            PQ[i] = low
            score = jnp.where(MSK[s] > 0, nt(low, PK[i]), 0.0).astype(BF)
            SS[i] = score
            MIX[i] = nn(score, VX[i])
            return carry

        lax.fori_loop(0, 3, body, 0, unroll=True)

    def mixing(s):
        tb_take(0, s, COMB)

        def body(h, carry):
            i = s * 3 + h
            cross = nt(PQ[i], COMB[i])
            numer = MIX[i] + jnp.where(CM[0, s] > 0, cross[:, 0:128], 0.0)
            numer = numer + jnp.where(CM[1, s] > 0, cross[:, 128:256], 0.0)
            denom = numer[:, 64:65]
            mixed = numer / denom
            MIX[i] = jnp.where(lanes_of((256, 128)) < 64, mixed, 0.0)
            DEN[i] = jnp.broadcast_to(denom, (256, 128))
            return carry

        lax.fori_loop(0, 3, body, 0, unroll=True)
        MIXC[s] = jnp.concatenate(
            [MIX[s * 3][:, 0:64], MIX[s * 3 + 1][:, 0:64], MIX[s * 3 + 2][:, 0:64]], axis=1
        ).astype(BF)

    def tb_desc(way, s, side, dist):
        heads = pl.ds(s * 3, 3)
        src = TBS.at[way, side, heads] if dist == 1 else TBR.at[way, side, 0, heads]
        return copy(
            src,
            TBR.at[way, side, dist - 1, heads],
            tb_s.at[way, s, side, dist - 1],
            tb_r.at[way, s, side, dist - 1],
            along(1 if side == 0 else 3),
        )

    def tb_send(way, s):
        for side in range(2):

            @pl.when(reaches(1 - side, 1))
            def _():
                tb_desc(way, s, side, 1).start()

    def tb_relay(way, s):
        for side in range(2):

            @pl.when(reaches(side, 1))
            def _():
                tb_desc(way, s, side, 1).wait_recv()

            @pl.when((z == 1) | (z == 2))
            def _():
                tb_desc(way, s, side, 2).start()

    def tb_take(way, s, comb):
        for side in range(2):

            @pl.when(reaches(side, 2))
            def _():
                tb_desc(way, s, side, 2).wait_recv()

            both = (edge(s, side, 1) == edge(s, side, 2)) & reaches(side, 2)
            both = jnp.broadcast_to(both, (TAB, 256))
            for h in range(3):
                i = s * 3 + h
                near = TBR[way, side, 0, i].astype(F32)
                total = near + jnp.where(both, TBR[way, side, 1, i].astype(F32), 0.0)
                comb[i, 128 * side : 128 * side + TAB, :] = total.astype(BF)

    def attn_out(s):
        P[s] = nt(MIXC[s], WO[...])

    gain_attn, shift_attn, gain_ffn, shift_ffn, bias_down = (
        ref[...].reshape(1, 768) for ref in (ga_ref, sa_ref, gf_ref, sf_ref, bd_ref)
    )
    ARS[0] = jnp.zeros((8, 768), F32)

    def add_small(row, value):
        ARS[0, row : row + 1, :] = ARS[0, row : row + 1, :] + value

    def over_rows(value):
        return jnp.sum(value, 0, keepdims=True)

    def norm_one(s, attn):
        normed, inv_std = norm_stats(x_ref[s].astype(F32) + attn)
        first = normed * gain_attn + shift_attn
        NORM1[s], FIRST[s] = normed, first
        INV1[s] = jnp.broadcast_to(inv_std, (64, 128))
        FI[s, chunk(t), :] = first.astype(BF)

    def norm_two(s, branch):
        normed, inv_std = norm_stats(FIRST[s] + branch + bias_down)
        out_ref[s] = (normed * gain_ffn + shift_ffn).astype(BF)
        cot = cot_ref[s].astype(F32)
        grad = norm_grad(cot, normed, inv_std, gain_ffn)
        GH2[s] = grad
        G2[s, chunk(t), :] = grad.astype(BF)
        add_small(2, over_rows(cot * normed))
        add_small(3, over_rows(cot))
        add_small(4, over_rows(grad))

    def norm_one_back(s, summed):
        grad_first = GH2[s] + summed
        normed = NORM1[s]
        grad = norm_grad(grad_first, normed, INV1[s][:, 0:1], gain_attn)
        GH1[s] = grad
        G1[s, chunk(t), :] = grad.astype(BF)
        add_small(0, over_rows(grad_first * normed))
        add_small(1, over_rows(grad_first))

    def tile(j):
        return pl.ds(pl.multiple_of(j * 256, 256), 256)

    def ffn_up(s):
        def body(j, carry):
            upper = nn(FI[s], WU[:, tile(j)]) + bu_ref[tile(j)].reshape(1, 256)
            cdf = 0.5 * (1.0 + lax.erf(upper * root_half))
            HID[s, :, tile(j)] = (upper * cdf).astype(BF)
            SLOPE[s, :, tile(j)] = cdf + upper * inv_root_tau * jnp.exp(-0.5 * upper * upper)
            return carry

        lax.fori_loop(0, 3, body, 0, unroll=True)

    def ffn_down(s):
        def body(j, carry):
            P[s, :, tile(j)] = nt(HID[s], WD[tile(j), :])
            return carry

        lax.fori_loop(0, 3, body, 0, unroll=True)

    def ffn_back_hidden(s):
        def body(j, carry):
            grad = (nn(G2[s], WD[:, tile(j)]) * SLOPE[s, :, tile(j)]).astype(BF)
            GUP[s, :, tile(j)] = grad
            ARS[0, 5:6, tile(j)] = ARS[0, 5:6, tile(j)] + over_rows(grad.astype(F32))
            return carry

        lax.fori_loop(0, 3, body, 0, unroll=True)

    def ffn_back_rows(s):
        def body(j, carry):
            P[s, :, tile(j)] = nt(GUP[s], WU[tile(j), :])
            return carry

        lax.fori_loop(0, 3, body, 0, unroll=True)

    def slots(i):
        narrow, wide = (GON, YSN, YRN, ZSN, ZRN), (GOW, YSW, YRW, ZSW, ZRW)
        return [ref.at[i] for ref in narrow] if i < 4 else [ref.at[i - 4] for ref in wide]

    def half_lanes(yy, j):
        return pl.ds(pl.multiple_of(yy * 384 + j * 128, 128), 128)

    def weight_part(left, right, yy, j):
        lanes = half_lanes(yy, j)
        return tn(left[0, :, lanes], right[0]) + tn(left[1, :, lanes], right[1])

    def half_rows(j):
        return pl.ds(pl.multiple_of(j * 128, 128), 128)

    def weight_send(i, left, right):
        sent = slots(i)[1]

        def other(j, carry):
            sent[half_rows(j), :] = weight_part(left, right, 1 - y, j).astype(BF)
            return carry

        lax.fori_loop(0, 3, other, 0)
        for n in range(4):
            block = (z + (2, 1, 3, 0)[n]) % 4 if i < 4 else n + (1 - z // 2) * (3 - 2 * n)
            gy_desc(i, block).start()

    def weight_keep(i, left, right):
        own_half = slots(i)[0]

        def here(j, carry):
            own_half[half_rows(j), :] = weight_part(left, right, y, j)
            return carry

        lax.fori_loop(0, 3, here, 0)

    def z_rows(block):
        return pl.ds(pl.multiple_of(block * 96, 96), 96)

    def gy_desc(i, block):
        sent, came_y = slots(i)[1:3]
        return copy(sent.at[z_rows(block), :], came_y.at[block], gy_s.at[i, block], gy_r.at[i, block], yp)

    def gz_desc(i, d):
        sent, came_z = slots(i)[3:5]
        return copy(sent.at[d - 1], came_z.at[d - 1], gz_s.at[i, d - 1], gz_r.at[i, d - 1], along(d))

    def chip_sum(i, block):
        own_half, _, came_y, _, _ = slots(i)
        gy_desc(i, block).wait_recv()
        return own_half[z_rows(block), :] + came_y[block].astype(F32)

    def g_pass(i):
        sent = slots(i)[3]
        for d in (2, 1, 3):
            sent[d - 1] = chip_sum(i, (z + d) % 4).astype(BF)
            gz_desc(i, d).start()

    def gc_desc(i, way, e):
        sent, came_z = ZSW.at[i - 4, way, e], ZRW.at[i - 4, way, e]
        return copy(sent, came_z, gc_s.at[i - 4, way, e], gc_r.at[i - 4, way, e], along(4 + step_of(way)))

    def gives(way, e):
        return z + e < 3 if way == 0 else z > e

    def behind(way):
        return z > 0 if way == 0 else z < 3

    def g_relay(i, e):
        for way in range(2):

            @pl.when(gives(way, e))
            def _():
                total = chip_sum(i, (z + 4 + (e + 1) * step_of(way)) % 4)
                ZSW[i - 4, way, e] = total.astype(BF)
                if e < 2:

                    @pl.when(behind(way))
                    def _():
                        gc_desc(i, way, e + 1).wait_recv()
                        ZSW[i - 4, way, e] = (total + ZRW[i - 4, way, e + 1].astype(F32)).astype(BF)

                gc_desc(i, way, e).start()

    def g_last(i, out):
        total = chip_sum(i, z)
        if i < 4:
            arrived = slots(i)[4]
            for d in (1, 2, 3):
                gz_desc(i, d).wait_recv()
                total = total + arrived[d - 1].astype(F32)
            out[...] = total
            return
        out[...] = total
        for way in range(2):

            @pl.when(behind(way))
            def _():
                gc_desc(i, way, 0).wait_recv()
                out[...] = out[...] + ZRW[i - 4, way, 0].astype(F32)

    def ar_desc(stage):
        where = (sib, far, yp)[stage]
        return copy(ARS.at[stage], ARR.at[stage], ar_s.at[stage], ar_r.at[stage], where)

    def ar_take(stage):
        ar_desc(stage).wait_recv()
        came = ARR[stage]
        if stage < 2:
            rows = lax.broadcasted_iota(jnp.int32, (8, 768), 0)
            came = jnp.where(rows < 5, came, 0.0)
        ARS[stage + 1] = ARS[stage] + came

    def ar_z_desc(i):
        return copy(ARS.at[3], ARZ.at[z], ar_s.at[3 + i], ar_r.at[3 + i], along(1 + i))

    def ar_z_start():
        ARZ[z] = ARS[3]
        for i in range(3):
            ar_z_desc(i).start()

    def ar_z_take():
        for i in range(3):
            ar_z_desc(i).wait_recv()
        small_ref[...] = (ARZ[0] + ARZ[1]) + (ARZ[2] + ARZ[3])

    def grad_tables(s):
        GM[...] = nn(G1[s], WO[...])
        lane = lanes_of((256, 128))
        zero = jnp.zeros((256, 64), F32)
        for h in range(3):
            i = s * 3 + h
            gm = jnp.concatenate([GM[:, 64 * h : 64 * h + 64], zero], axis=1)
            denom = DEN[i]
            slope = -jnp.sum(gm * MIX[i], -1, keepdims=True) / denom
            s_hi = slope.astype(BF).astype(F32)
            ext = jnp.where(lane == 64, s_hi, gm / denom)
            GX[i] = jnp.where(lane == 65, slope - s_hi, ext).astype(BF)

        def body(h, carry):
            i = s * 3 + h
            made = tables(GX[i], PQ[i], s)
            TBS[1, 1, i] = made[0:TAB].astype(BF)
            TBS[1, 0, i] = made[TAB : 2 * TAB].astype(BF)
            return carry

        lax.fori_loop(0, 3, body, 0, unroll=True)

    def pair(ext, s):
        ext = ext.astype(F32)
        return jnp.concatenate([ext * CM[0, s], ext * CM[1, s]], axis=1).astype(BF)

    def through_phi(grad_phi, phi, scaled, h):
        both = nn((grad_phi * phi).astype(BF), OMT[h])
        both = both[:, 0:128] + both[:, 128:256]
        return (both - scaled * both[:, 64:65]) * HEAD_DIM ** (-0.25)

    def side_by_side(heads):
        return jnp.concatenate([heads[h][:, 0:64] for h in range(3)], axis=1).astype(BF)

    def back_queries(s):
        def body(h, carry):
            i = s * 3 + h
            ext = GX[i]
            pairs = jnp.where(MSK[s] > 0, nt(ext, VX[i]), 0.0).astype(BF)
            grad = nn(pairs, PK[i]) + nn(pair(ext, s), COMB[i])
            GM3[h] = through_phi(grad, PQF[i], RQ[i], h)
            GKL[i] = tn(pairs, PQ[i])
            GVL[i] = tn(SS[i], ext)
            return carry

        lax.fori_loop(0, 3, body, 0, unroll=True)
        RGQ[s] = side_by_side(GM3)

    def back_keys(s):
        tb_take(1, s, GCOMB)

        def body(h, carry):
            i = s * 3 + h
            grad = GKL[i] + nn(pair(VX[i], s), GCOMB[i])
            GM3[h] = through_phi(grad, PKF[i], RK[i], h)
            cross = nt(PK[i], GCOMB[i])
            gv = GVL[i] + jnp.where(CM[0, s] > 0, cross[:, 0:128], 0.0)
            GV3[h] = gv + jnp.where(CM[1, s] > 0, cross[:, 128:256], 0.0)
            return carry

        lax.fori_loop(0, 3, body, 0, unroll=True)
        RGK[s] = side_by_side(GM3)
        RGV[s] = side_by_side(GV3)

    def input_rows(s):
        def body(j, carry):
            made = nt(RGQ[s], WQ[tile(j), :]) + nt(RGK[s], WK[tile(j), :])
            P[s, :, tile(j)] = made + nt(RGV[s], WV[tile(j), :])
            return carry

        lax.fori_loop(0, 3, body, 0, unroll=True)

    w_send(4)
    w_send(3)
    w_send(5)
    w_pass(2)
    w_over(3)
    w_over(4)
    w_over(5)
    w_wait(0)
    w_wait(1)
    ag_wait(0, X, 0)
    project_keys(0)
    keys(0)
    tb_send(0, 0)
    ag_wait(0, X, 1)
    project_keys(1)
    keys(1)
    tb_send(0, 1)
    w_pass(3)
    w_wait(2)
    project_queries(0)
    queries(0)
    tb_relay(0, 0)
    project_queries(1)
    queries(1)
    tb_relay(0, 1)
    w_relay(4, 0)
    w_relay(5, 0)
    mixing(0)
    w_wait(3)
    attn_out(0)
    rs_start(0, 0)
    mixing(1)
    attn_out(1)
    rs_mid(0, 0)
    rs_start(0, 1)
    w_relay(4, 1)
    rs_mid(0, 1)
    norm_one(0, rs_fin(0, 0))
    ag_start(1, FI, 0)
    w_relay(5, 1)
    norm_one(1, rs_fin(0, 1))
    ag_start(1, FI, 1)
    w_relay(4, 2)
    ag_pass(1, FI, 0)
    ag_wait(1, FI, 0)
    w_relay(5, 2)
    w_wait(4)
    ffn_up(0)
    ag_pass(1, FI, 1)
    ag_wait(1, FI, 1)
    ffn_up(1)
    w_wait(5)
    ffn_down(0)
    rs_start(1, 0)
    ffn_down(1)
    rs_mid(1, 0)
    rs_start(1, 1)
    rs_mid(1, 1)
    norm_two(0, rs_fin(1, 0))
    ag_start(2, G2, 0)
    norm_two(1, rs_fin(1, 1))
    ag_start(2, G2, 1)
    ag_pass(2, G2, 0)
    ag_wait(2, G2, 0)
    ffn_back_hidden(0)
    ag_pass(2, G2, 1)
    ffn_back_rows(0)
    rs_start(2, 0)
    ag_wait(2, G2, 1)
    weight_send(5, G2, HID)
    rs_mid(2, 0)
    ffn_back_hidden(1)
    ffn_back_rows(1)
    rs_start(2, 1)
    weight_send(4, FI, GUP)
    rs_mid(2, 1)
    norm_one_back(0, rs_fin(2, 0))
    ag_start(3, G1, 0)
    weight_keep(5, G2, HID)
    norm_one_back(1, rs_fin(2, 1))
    ag_start(3, G1, 1)
    ar_desc(0).start()
    g_relay(5, 2)
    ag_pass(3, G1, 0)
    weight_keep(4, FI, GUP)
    ag_wait(3, G1, 0)
    grad_tables(0)
    tb_send(1, 0)
    ag_pass(3, G1, 1)
    ar_take(0)
    ar_desc(1).start()
    ag_wait(3, G1, 1)
    grad_tables(1)
    tb_send(1, 1)
    weight_send(3, G1, MIXC)
    g_relay(5, 1)
    back_queries(0)
    tb_relay(1, 0)
    ar_take(1)
    ar_desc(2).start()
    back_queries(1)
    tb_relay(1, 1)
    weight_send(2, X, RGQ)
    g_relay(5, 0)
    weight_keep(3, G1, MIXC)
    weight_keep(2, X, RGQ)
    ar_take(2)
    ar_z_start()
    g_relay(4, 2)
    back_keys(0)
    input_rows(0)
    rs_start(3, 0)
    g_relay(4, 1)
    back_keys(1)
    rs_mid(3, 0)
    weight_send(0, X, RGK)
    weight_send(1, X, RGV)
    input_rows(1)
    rs_start(3, 1)
    g_pass(3)
    weight_keep(0, X, RGK)
    weight_keep(1, X, RGV)
    g_relay(4, 0)
    rs_mid(3, 1)
    g_pass(2)
    g_pass(0)
    g_pass(1)
    gin_ref[0] = (GH1[0] + rs_fin(3, 0)).astype(BF)
    gin_ref[1] = (GH1[1] + rs_fin(3, 1)).astype(BF)
    ar_z_take()
    g_last(5, od_ref)
    g_last(4, ou_ref)
    g_last(3, oo_ref)
    g_last(2, oq_ref)
    g_last(0, ok_ref)
    g_last(1, ov_ref)

    for s in range(2):
        for op, buf in enumerate((X, FI, G2, G1)):
            for which in range(3):
                ag_desc(op, buf, s, which).wait_send()
        for op in range(4):
            sib_desc(op, s, 0).wait_send()
            sib_desc(op, s, 1).wait_send()
            xrs_desc(op, s).wait_send()
        for way in range(2):
            for side in range(2):

                @pl.when(reaches(1 - side, 1))
                def _():
                    tb_desc(way, s, side, 1).wait_send()

                @pl.when((z == 1) | (z == 2))
                def _():
                    tb_desc(way, s, side, 2).wait_send()

    for i in range(6):
        wy_desc(i, 0).wait_send()
        for block in range(4):
            gy_desc(i, block).wait_send()
        for d in (1, 2, 3):
            if i < 4:
                wy_desc(i, d).wait_send()
                wz_desc(i, d).wait_send()
                gz_desc(i, d).wait_send()
    for i in (4, 5):
        for way in range(2):
            for j in range(3):

                @pl.when(goes(way, j))
                def _():
                    wc_desc(i, way, j).wait_send()

                @pl.when(came(way, j))
                def _():
                    wf_desc(i, way, j).wait_send()

                @pl.when(gives(way, j))
                def _():
                    gc_desc(i, way, j).wait_send()

    for stage in range(3):
        ar_desc(stage).wait_send()
        ar_z_desc(stage).wait_send()
        seg_desc(stage + 1).wait_send()


def hand_out(
    out_ref, gin_ref, ok_ref, ov_ref, oq_ref, oo_ref, ou_ref, od_ref, small_ref,
    out_o, gin_o, q_o, k_o, v_o, o_o, ga_o, sa_o, u_o, bu_o, d_o, bd_o, gf_o, sf_o,
):
    narrow = ((q_o, oq_ref), (k_o, ok_ref), (v_o, ov_ref))
    for dst, src in narrow + ((out_o, out_ref), (gin_o, gin_ref), (u_o, ou_ref), (d_o, od_ref)):
        dst[...] = src[...]
    o_o[...] = oo_ref[...].T
    for row, dst in enumerate((ga_o, sa_o, gf_o, sf_o, bd_o, bu_o)):
        dst[...] = small_ref[row, :]


def dma(*shape):
    return pltpu.SemaphoreType.DMA(shape)


def fast_device(
    inputs, seg_ids, feature_map, w_query, w_key, w_value, w_out, gain_attn, shift_attn,
    w_up, bias_up, w_down, bias_down, gain_ffn, shift_ffn, cotangent,
):
    vm = pltpu.VMEM
    scratch = [
        vm((2, 256, 768), BF), vm((2, 256, 768), BF), vm((2, 256, 768), BF), vm((2, 256, 768), BF),
        vm((768, 192), BF), vm((768, 192), BF), vm((768, 192), BF), vm((768, 192), BF),
        vm((768, 768), BF), vm((768, 768), BF), vm((96, 192), BF),
        vm((2, 256, 768), F32), vm((2, 256, 768), BF), vm((2, 256, 768), F32), vm((2, 256, 768), BF),
        vm((2, 64, 768), F32), vm((2, 64, 768), F32), vm((2, 64, 128), F32),
        vm((2, 64, 768), F32), vm((2, 64, 768), F32),
        vm((6, 256, 128), F32), vm((6, 256, 128), F32), vm((6, 256, 128), BF),
        vm((6, 256, 256), F32), vm((6, 256, 256), F32), vm((6, 256, 256), BF), vm((6, 256, 256), BF),
        vm((6, 256, 256), BF),
        vm((2, 256, 256), F32), vm((2, 2, 256, 128), F32), vm((4, 2, 256), jnp.int32),
        vm((3, 256, 256), BF), vm((3, 128, 256), BF), vm((3, 256, 256), BF),
        vm((6, 256, 128), F32), vm((6, 256, 128), F32), vm((6, 256, 128), BF),
        vm((6, 256, 256), F32), vm((6, 256, 128), F32),
        vm((256, 192), F32), vm((3, 256, 128), F32), vm((3, 256, 128), F32),
        vm((2, 256, 192), BF), vm((2, 256, 192), BF), vm((2, 256, 192), BF), vm((2, 256, 192), BF),
        vm((2, 2, 6, TAB, 256), BF), vm((2, 2, 2, 6, TAB, 256), BF), vm((6, 256, 256), BF), vm((6, 256, 256), BF),
        vm((4, 2, 2, 64, 768), BF), vm((4, 2, 2, 64, 768), BF), vm((4, 2, 64, 768), BF), vm((4, 2, 64, 768), BF),
        vm((4, 384, 192), F32), vm((2, 384, 768), F32),
        vm((4, 384, 192), BF), vm((2, 384, 768), BF),
        vm((4, 4, 96, 192), BF), vm((2, 4, 96, 768), BF),
        vm((4, 3, 96, 192), BF), vm((2, 2, 3, 96, 768), BF),
        vm((4, 3, 96, 192), BF), vm((2, 2, 3, 96, 768), BF),
        vm((4, 8, 768), F32), vm((3, 8, 768), F32), vm((4, 8, 768), F32),
        dma(4, 2, 3), dma(4, 2, 3), dma(4, 2, 3), dma(4, 2, 3), dma(3), dma(3),
        dma(4, 3), dma(4, 3), dma(6, 4), dma(6, 4), dma(2, 2, 3), dma(2, 2, 3), dma(2, 2, 3), dma(2, 2, 3),
        dma(6, 4), dma(6, 4), dma(4, 3), dma(4, 3), dma(2, 2, 3), dma(2, 2, 3),
        dma(2, 2, 2, 2), dma(2, 2, 2, 2), dma(6), dma(6),
    ]
    in_vmem = pl.BlockSpec(memory_space=pltpu.VMEM)
    shape = jax.ShapeDtypeStruct
    narrow, wide, rows, vec = shape((96, 192), F32), shape((96, 768), F32), shape((2, 64, 768), BF), shape((768,), F32)
    made = pl.pallas_call(
        layer_kernel,
        out_shape=(rows, rows, narrow, narrow, narrow, narrow, wide, wide, shape((8, 768), F32)),
        in_specs=[in_vmem] * 16,
        out_specs=(in_vmem,) * 9,
        scratch_shapes=scratch,
        compiler_params=pltpu.CompilerParams(
            collective_id=0, has_side_effects=True, vmem_limit_bytes=67043328
        ),
    )(
        inputs, seg_ids, feature_map, w_query, w_key, w_value, w_out, gain_attn, shift_attn,
        w_up, bias_up, w_down.T, bias_down, gain_ffn, shift_ffn, cotangent,
    )
    done = pl.pallas_call(
        hand_out,
        out_shape=(
            rows, rows, narrow, narrow, narrow, shape((192, 96), F32), vec, vec,
            wide, vec, wide, vec, vec, vec,
        ),
        in_specs=[in_vmem] * 9,
        out_specs=(in_vmem,) * 14,
    )(*made)
    return (*done[:10], done[10].T, *done[11:])


def solution(mesh):
    placed = (
        P("shard", ("ctx", "tp"), None),
        P("shard", "ctx"),
        P("tp", None, None),
        P(("shard", "ctx"), "tp"),
        P(("shard", "ctx"), "tp"),
        P(("shard", "ctx"), "tp"),
        P("tp", ("shard", "ctx")),
        P(),
        P(),
        P(("shard", "ctx"), "tp"),
        P("tp"),
        P("tp", ("shard", "ctx")),
        P(),
        P(),
        P(),
        P("shard", ("ctx", "tp"), None),
    )
    sizes = tuple(mesh.shape[axis] for axis in ("shard", "ctx", "tp"))
    return jax.shard_map(
        fast_device if sizes == (2, 4, 4) else per_device,
        mesh=mesh,
        in_specs=placed,
        out_specs=(
            P("shard", ("ctx", "tp"), None),
            P("shard", ("ctx", "tp"), None),
            P(("shard", "ctx"), "tp"),
            P(("shard", "ctx"), "tp"),
            P(("shard", "ctx"), "tp"),
            P("tp", ("shard", "ctx")),
            P(),
            P(),
            P(("shard", "ctx"), "tp"),
            P("tp"),
            P("tp", ("shard", "ctx")),
            P(),
            P(),
            P(),
        ),
        check_vma=False,
    )
```

```python
import jax
import jax.numpy as jnp
from jax import lax
from jax.experimental import pallas as pl
from jax.experimental.pallas import tpu as pltpu
from jax.sharding import PartitionSpec as P

HEAD_DIM = 64
FEATS = 256
FF = 3072
SEGS = 8


highest = lax.Precision.HIGHEST
root_half = 0.7071067811865476
inv_root_tau = 0.3989422804014327
norm_eps = 1e-05


def gelu_value(upper):
    return upper * 0.5 * (1.0 + lax.erf(upper * root_half))


def gelu_slope(upper):
    return 0.5 * (1.0 + lax.erf(upper * root_half)) + upper * inv_root_tau * jnp.exp(
        -0.5 * upper * upper
    )


def layer_norm(hidden_in, gain_vec, shift_vec):
    mean_val = jnp.mean(hidden_in, -1, keepdims=True)
    centred = hidden_in - mean_val
    inv_std = lax.rsqrt(jnp.mean(centred * centred, -1, keepdims=True) + norm_eps)
    normed = centred * inv_std
    return (normed * gain_vec + shift_vec, normed, inv_std)


def norm_back(grad_in, normed, inv_std, gain_vec):
    scaled = grad_in * gain_vec
    grad_hidden = inv_std * (
        scaled
        - jnp.mean(scaled, -1, keepdims=True)
        - normed * jnp.mean(scaled * normed, -1, keepdims=True)
    )
    return (grad_hidden, jnp.sum(grad_in * normed, (0, 1)), jnp.sum(grad_in, (0, 1)))


def features(projected, omega_local):
    seq_count, ctx_rows, width = projected.shape
    heads_here = omega_local.shape[0]
    scaled = projected.reshape(seq_count, ctx_rows, heads_here, HEAD_DIM) * HEAD_DIM ** (-0.25)
    angles = jnp.einsum("schd,hdm->schm", scaled, omega_local, precision=highest)
    squares = 0.5 * jnp.sum(scaled * scaled, -1, keepdims=True)
    return (jnp.exp(angles - squares) * FEATS ** (-0.5), scaled)


def feature_back(grad_phi, phi_full, scaled, omega_local):
    grad_angle = grad_phi * phi_full
    grad_scaled = jnp.einsum("schm,hdm->schd", grad_angle, omega_local, precision=highest)
    grad_scaled = grad_scaled - scaled * jnp.sum(grad_angle, -1, keepdims=True)
    seq_count, ctx_rows, heads_here, head_width = scaled.shape
    return (grad_scaled * HEAD_DIM ** (-0.25)).reshape(seq_count, ctx_rows, heads_here * head_width)


def spread_rows(mask_low, left):
    ctx_rows, heads_here, feat_count = left.shape
    wide = mask_low[:, None, :, None] * left[:, :, None, :]
    return wide.reshape(ctx_rows, heads_here, -1)


def segment_outer(operands):
    mask_low, left, right = operands
    return jnp.einsum(
        "chx,che->hxe", spread_rows(mask_low, left), right, preferred_element_type=jnp.float32
    )


def segment_apply(operands):
    mask_low, left, table = operands
    return jnp.einsum(
        "chx,hxe->che", spread_rows(mask_low, left), table, preferred_element_type=jnp.float32
    )


def segment_back(operands):
    mask_full, left, table = operands
    ctx_rows, heads_here, width = left.shape
    seg_count = mask_full.shape[1]
    wide = jnp.einsum("che,hxe->chx", left, table, preferred_element_type=jnp.float32)
    wide = wide.reshape(ctx_rows, heads_here, seg_count, -1)
    return jnp.sum(wide * mask_full[:, None, :, None], 2)


def inner_product(left, right):
    return lax.dot_general(
        left, right, (((0,), (0,)), ((), ())), preferred_element_type=jnp.float32
    )


def right_transposed(left, right):
    return lax.dot_general(
        left, right, (((1,), (1,)), ((), ())), preferred_element_type=jnp.float32
    )


def per_device(
    inputs,
    seg_ids,
    feature_map,
    w_query,
    w_key,
    w_value,
    w_out,
    gain_attn,
    shift_attn,
    w_up,
    bias_up,
    w_down,
    bias_down,
    gain_ffn,
    shift_ffn,
    cotangent,
):
    full_query, full_key, full_value, full_up, full_out, full_down = (
        lax.all_gather(w_query, ("shard", "ctx"), axis=0, tiled=True),
        lax.all_gather(w_key, ("shard", "ctx"), axis=0, tiled=True),
        lax.all_gather(w_value, ("shard", "ctx"), axis=0, tiled=True),
        lax.all_gather(w_up, ("shard", "ctx"), axis=0, tiled=True),
        lax.all_gather(w_out, ("shard", "ctx"), axis=1, tiled=True),
        lax.all_gather(w_down, ("shard", "ctx"), axis=1, tiled=True),
    )
    seq_count, row_share, width = inputs.shape
    rows_all = lax.all_gather(inputs, "tp", axis=1, tiled=True)
    ctx_rows = rows_all.shape[1]
    token_count = seq_count * ctx_rows
    flat = rows_all.reshape(token_count, width)
    heads_here = feature_map.shape[0]
    head_cols = heads_here * HEAD_DIM
    query_proj = jnp.dot(flat, full_query, preferred_element_type=jnp.float32).reshape(
        seq_count, ctx_rows, head_cols
    )
    key_proj = jnp.dot(flat, full_key, preferred_element_type=jnp.float32).reshape(
        seq_count, ctx_rows, head_cols
    )
    value_low = jnp.dot(flat, full_value, preferred_element_type=jnp.float32).astype(jnp.bfloat16)
    value_low = value_low.reshape(seq_count, ctx_rows, head_cols)
    value_four = value_low.reshape(seq_count, ctx_rows, heads_here, HEAD_DIM)
    phi_query, scaled_query = features(query_proj, feature_map)
    phi_key, scaled_key = features(key_proj, feature_map)
    phq_low = phi_query.astype(jnp.bfloat16)
    phk_low = phi_key.astype(jnp.bfloat16)
    matches = seg_ids[:, :, None] == jnp.arange(SEGS, dtype=jnp.int32)[None, None, :]
    mask_low = matches.astype(jnp.bfloat16)
    mask_full = matches.astype(jnp.float32)
    kv_part = lax.map(segment_outer, (mask_low, phk_low, value_four))
    z_part = jnp.einsum("scg,schm->shgm", mask_low, phk_low, preferred_element_type=jnp.float32)
    kv_sum, z_sum = lax.psum((kv_part, z_part), "ctx")
    kv_low = kv_sum.astype(jnp.bfloat16)
    numer = lax.map(segment_apply, (mask_low, phq_low, kv_low))
    phq_wide = phq_low.astype(jnp.float32)
    denom = jnp.sum(
        jnp.einsum("schm,shgm->schg", phq_wide, z_sum, precision=highest)
        * mask_full[:, :, None, :],
        -1,
    )
    mixed = numer / denom[..., None]
    mixed_low = mixed.astype(jnp.bfloat16).reshape(seq_count, ctx_rows, head_cols)
    piece = mixed_low
    attn_sum = jnp.swapaxes(
        lax.psum_scatter(
            jnp.einsum("scf,fd->csd", piece, full_out, preferred_element_type=jnp.float32),
            "tp",
            scatter_dimension=0,
            tiled=True,
        ),
        0,
        1,
    )
    first, normed_one, inv_one = layer_norm(
        inputs.astype(jnp.float32) + attn_sum, gain_attn, shift_attn
    )
    first_low = first.astype(jnp.bfloat16)
    first_rows = lax.all_gather(first_low, "tp", axis=1, tiled=True)
    first_flat = first_rows.reshape(token_count, width)
    upper = jnp.dot(first_flat, full_up, preferred_element_type=jnp.float32) + bias_up
    ffn_here = upper.shape[1]
    hidden_low = gelu_value(upper).astype(jnp.bfloat16)
    hidden_three = hidden_low.reshape(seq_count, ctx_rows, ffn_here)
    piece = hidden_three
    branch = jnp.swapaxes(
        lax.psum_scatter(
            jnp.einsum("scf,fd->csd", piece, full_down, preferred_element_type=jnp.float32),
            "tp",
            scatter_dimension=0,
            tiled=True,
        ),
        0,
        1,
    )
    final, normed_two, inv_two = layer_norm(first + branch + bias_down, gain_ffn, shift_ffn)
    outputs = final.astype(jnp.bfloat16)
    full_query, full_key, full_value, full_up, full_out, full_down = (
        lax.all_gather(w_query, ("shard", "ctx"), axis=0, tiled=True),
        lax.all_gather(w_key, ("shard", "ctx"), axis=0, tiled=True),
        lax.all_gather(w_value, ("shard", "ctx"), axis=0, tiled=True),
        lax.all_gather(w_up, ("shard", "ctx"), axis=0, tiled=True),
        lax.all_gather(w_out, ("shard", "ctx"), axis=1, tiled=True),
        lax.all_gather(w_down, ("shard", "ctx"), axis=1, tiled=True),
    )
    grad_final = cotangent.astype(jnp.float32)
    grad_two, grad_gain_ffn, grad_shift_ffn = norm_back(grad_final, normed_two, inv_two, gain_ffn)
    grad_bias_down = jnp.sum(grad_two, (0, 1))
    grad_two_rows = lax.all_gather(grad_two.astype(jnp.bfloat16), "tp", axis=1, tiled=True)
    grad_two_flat = grad_two_rows.reshape(token_count, width)
    grad_hidden = right_transposed(grad_two_flat, full_down)
    grad_upper = (grad_hidden * gelu_slope(upper)).astype(jnp.bfloat16)
    grad_down = inner_product(hidden_low, grad_two_flat)
    grad_up = inner_product(first_flat, grad_upper)
    grad_bias_local = jnp.sum(grad_upper.astype(jnp.float32), 0)
    grad_upper_three = grad_upper.reshape(seq_count, ctx_rows, ffn_here)
    piece = grad_upper_three
    grad_first = grad_two + jnp.swapaxes(
        lax.psum_scatter(
            jnp.einsum("scf,df->csd", piece, full_up, preferred_element_type=jnp.float32),
            "tp",
            scatter_dimension=0,
            tiled=True,
        ),
        0,
        1,
    )
    grad_one, grad_gain_attn, grad_shift_attn = norm_back(
        grad_first, normed_one, inv_one, gain_attn
    )
    grad_one_rows = lax.all_gather(grad_one.astype(jnp.bfloat16), "tp", axis=1, tiled=True)
    grad_one_flat = grad_one_rows.reshape(token_count, width)
    grad_out = inner_product(mixed_low.reshape(token_count, head_cols), grad_one_flat)
    grad_mixed = right_transposed(grad_one_flat, full_out).reshape(
        seq_count, ctx_rows, heads_here, HEAD_DIM
    )
    grad_numer = (grad_mixed / denom[..., None]).astype(jnp.bfloat16)
    grad_denom = -jnp.sum(grad_mixed * mixed, -1) / denom
    kv_grad_part = lax.map(segment_outer, (mask_low, phq_low, grad_numer))
    z_grad_part = jnp.einsum(
        "scg,schm->shgm", mask_full, phq_wide * grad_denom[..., None], precision=highest
    )
    kv_grad, z_grad = (
        lax.psum(kv_grad_part.astype(jnp.bfloat16), "ctx").astype(jnp.float32),
        lax.psum(z_grad_part.astype(jnp.bfloat16), "ctx").astype(jnp.float32),
    )
    kv_grad_low = kv_grad.astype(jnp.bfloat16)
    grad_phq = lax.map(segment_back, (mask_full, grad_numer, kv_low))
    grad_phq = grad_phq + grad_denom[..., None] * jnp.einsum(
        "scg,shgm->schm", mask_full, z_sum, precision=highest
    )
    grad_phk = lax.map(segment_back, (mask_full, value_four, kv_grad_low))
    grad_phk = grad_phk + jnp.einsum("scg,shgm->schm", mask_full, z_grad, precision=highest)
    grad_value_rows = lax.map(segment_apply, (mask_low, phk_low, kv_grad_low)).astype(jnp.bfloat16)
    grad_value_rows = grad_value_rows.reshape(seq_count, ctx_rows, head_cols)
    grad_query_rows = feature_back(grad_phq, phi_query, scaled_query, feature_map).astype(
        jnp.bfloat16
    )
    grad_key_rows = feature_back(grad_phk, phi_key, scaled_key, feature_map).astype(jnp.bfloat16)
    grad_query = inner_product(flat, grad_query_rows.reshape(token_count, head_cols))
    grad_key = inner_product(flat, grad_key_rows.reshape(token_count, head_cols))
    grad_value = inner_product(flat, grad_value_rows.reshape(token_count, head_cols))
    total = jnp.einsum(
        "scf,df->csd", grad_query_rows, full_query, preferred_element_type=jnp.float32
    )
    total = total + jnp.einsum(
        "scf,df->csd", grad_key_rows, full_key, preferred_element_type=jnp.float32
    )
    grad_rows = jnp.swapaxes(
        lax.psum_scatter(
            (
                total
                + jnp.einsum(
                    "scf,df->csd", grad_value_rows, full_value, preferred_element_type=jnp.float32
                )
            ).astype(jnp.bfloat16),
            "tp",
            scatter_dimension=0,
            tiled=True,
        ).astype(jnp.float32),
        0,
        1,
    )
    grad_inputs = (grad_one + grad_rows).astype(jnp.bfloat16)
    grad_query, grad_key, grad_value, grad_up, grad_out, grad_down = (
        lax.psum_scatter(grad_query, ("shard", "ctx"), scatter_dimension=0, tiled=True),
        lax.psum_scatter(grad_key, ("shard", "ctx"), scatter_dimension=0, tiled=True),
        lax.psum_scatter(grad_value, ("shard", "ctx"), scatter_dimension=0, tiled=True),
        lax.psum_scatter(grad_up, ("shard", "ctx"), scatter_dimension=0, tiled=True),
        lax.psum_scatter(grad_out, ("shard", "ctx"), scatter_dimension=1, tiled=True),
        lax.psum_scatter(grad_down, ("shard", "ctx"), scatter_dimension=1, tiled=True),
    )
    tp_index = lax.axis_index("tp")
    padded_bias = lax.dynamic_update_slice(
        jnp.zeros((FF,), jnp.float32), grad_bias_local, (tp_index * ffn_here,)
    )
    grad_gain_attn, grad_shift_attn, grad_gain_ffn, grad_shift_ffn, grad_bias_down, padded_bias = (
        lax.psum(
            (
                grad_gain_attn,
                grad_shift_attn,
                grad_gain_ffn,
                grad_shift_ffn,
                grad_bias_down,
                padded_bias,
            ),
            ("shard", "ctx", "tp"),
        )
    )
    grad_bias_up = lax.dynamic_slice(padded_bias, (tp_index * ffn_here,), (ffn_here,))
    return (
        outputs,
        grad_inputs,
        grad_query,
        grad_key,
        grad_value,
        grad_out,
        grad_gain_attn,
        grad_shift_attn,
        grad_up,
        grad_bias_up,
        grad_down,
        grad_bias_down,
        grad_gain_ffn,
        grad_shift_ffn,
    )


BF = jnp.bfloat16
F32 = jnp.float32
MESH_ID = pl.DeviceIdType.MESH
TAB = 80
SUBS = 3


def nn(left, right):
    return lax.dot_general(left, right, (((1,), (0,)), ((), ())), preferred_element_type=F32)


def nt(left, right):
    return lax.dot_general(left, right, (((1,), (1,)), ((), ())), preferred_element_type=F32)


def tn(left, right):
    return lax.dot_general(left, right, (((0,), (0,)), ((), ())), preferred_element_type=F32)


def lanes_of(shape):
    return lax.broadcasted_iota(jnp.int32, shape, 1)


def norm_stats(hidden_in):
    centred = hidden_in - jnp.mean(hidden_in, -1, keepdims=True)
    inv_std = lax.rsqrt(jnp.mean(centred * centred, -1, keepdims=True) + norm_eps)
    return centred * inv_std, inv_std


def norm_grad(grad_in, normed, inv_std, gain_vec):
    scaled = grad_in * gain_vec
    return inv_std * (
        scaled
        - jnp.mean(scaled, -1, keepdims=True)
        - normed * jnp.mean(scaled * normed, -1, keepdims=True)
    )


def layer_kernel(
    x_ref, seg_ref, om_ref, wq_ref, wk_ref, wv_ref, wo_ref, ga_ref, sa_ref, wu_ref, bu_ref, wd_ref,
    bd_ref, gf_ref, sf_ref, cot_ref,
    out_ref, gin_ref, ok_ref, ov_ref, oq_ref, oo_ref, ou_ref, od_ref, small_ref,
    X, FI, G2, G1, WK, WV, WQ, WO, WU, WD, OWN_O, P, HID, SLOPE, GUP,
    FIRST, NORM1, INV1, GH2, GH1,
    RQ, RK, VX, PQF, PKF, PQ, PK, SS, MSK, CM, SEGZ,
    OM1, OM2, OMT,
    MIX, DEN, GX, GKL, GVL, GM, GM3, GV3, RGK, RGV, RGQ, MIXC,
    TBS, TBR, COMB, GCOMB,
    SIBS, SIBR, XS, XR,
    GON, GOW, YSN, YSW, YRN, YRW, ZSN, ZSW, ZRN, ZRW,
    ARS, ARR, ARZ,
    ag_s, ag_r, ra_s, ra_r, seg_s, seg_r, wz_s, wz_r, wy_s, wy_r, wc_s, wc_r, wf_s, wf_r, gy_s, gy_r, gz_s, gz_r, gc_s, gc_r, tb_s, tb_r, ar_s, ar_r,
):
    y = lax.axis_index("shard")
    z = lax.axis_index("ctx")
    t = lax.axis_index("tp")
    sib_t, far_t = t + 1 - 2 * (t % 2), 3 - t
    sib = {"tp": sib_t}
    far = {"tp": far_t}
    yp = {"shard": 1 - y}

    def along(d):
        return {"ctx": (z + d) % 4}

    def block_rows(yy, zz):
        return pl.ds(pl.multiple_of((yy * 4 + zz) * 96, 96), 96)

    def copy(src, dst, send, recv, where):
        return pltpu.make_async_remote_copy(
            src_ref=src, dst_ref=dst, send_sem=send, recv_sem=recv, device_id=where,
            device_id_type=MESH_ID,
        )

    barrier = pltpu.get_barrier_semaphore()
    for where in (sib, far, yp, along(1), along(2), along(3)):
        pl.semaphore_signal(barrier, inc=1, device_id=where, device_id_type=MESH_ID)
    pl.semaphore_wait(barrier, 6)

    def chunk(tt):
        return pl.ds(pl.multiple_of(tt * 64, 64), 64)

    def ag_desc(op, buf, s, which):
        rows = chunk(far_t) if which == 2 else chunk(t)
        where = far if which == 1 else sib
        return copy(
            buf.at[s, rows, :], buf.at[s, rows, :], ag_s.at[op, s, which], ag_r.at[op, s, which], where
        )

    def ag_start(op, buf, s):
        ag_desc(op, buf, s, 1).start()
        ag_desc(op, buf, s, 0).start()

    def ag_pass(op, buf, s):
        ag_desc(op, buf, s, 1).wait_recv()
        ag_desc(op, buf, s, 2).start()

    def ag_wait(op, buf, s):
        ag_desc(op, buf, s, 0).wait_recv()
        ag_desc(op, buf, s, 2).wait_recv()

    def sib_desc(op, s, part):
        return copy(
            SIBS.at[op, s, part], SIBR.at[op, s, part], ra_s.at[op, s, part], ra_r.at[op, s, part], sib
        )

    def xrs_desc(op, s):
        return copy(XS.at[op, s], XR.at[op, s], ra_s.at[op, s, 2], ra_r.at[op, s, 2], far)

    def part_rows(s, tt):
        return P[s, chunk(tt), :]

    def rs_start(op, s):
        SIBS[op, s, 0] = part_rows(s, (t + 2) % 4).astype(BF)
        sib_desc(op, s, 0).start()
        SIBS[op, s, 1] = part_rows(s, sib_t).astype(BF)
        sib_desc(op, s, 1).start()

    def rs_mid(op, s):
        sib_desc(op, s, 0).wait_recv()
        XS[op, s] = (part_rows(s, far_t) + SIBR[op, s, 0].astype(F32)).astype(BF)
        xrs_desc(op, s).start()

    def rs_fin(op, s):
        sib_desc(op, s, 1).wait_recv()
        kept = part_rows(s, t) + SIBR[op, s, 1].astype(F32)
        xrs_desc(op, s).wait_recv()
        return kept + XR[op, s].astype(F32)

    gathered = (WK, WV, WQ, WO, WU, WD)
    mine = (wk_ref, wv_ref, wq_ref, OWN_O, wu_ref, wd_ref)

    def wz_desc(i, d):
        dst = gathered[i].at[block_rows(y, z), :]
        return copy(mine[i], dst, wz_s.at[i, d - 1], wz_r.at[i, d - 1], along(d))

    def wy_desc(i, d):
        dst = gathered[i].at[block_rows(y, (z + 4 - d) % 4), :]
        return copy(mine[i] if d == 0 else dst, dst, wy_s.at[i, d], wy_r.at[i, d], yp)

    def step_of(way):
        return 1 - 2 * way

    def came(way, j):
        return z > j if way == 0 else z + j < 3

    def goes(way, j):
        return (z >= j) & (z < 3) if way == 0 else (z + j <= 3) & (z > 0)

    def wc_desc(i, way, j):
        dst = gathered[i].at[block_rows(y, (z + 4 - j * step_of(way)) % 4), :]
        src = mine[i] if j == 0 else dst
        return copy(src, dst, wc_s.at[i - 4, way, j], wc_r.at[i - 4, way, j], along(4 + step_of(way)))

    def wf_desc(i, way, j):
        part = gathered[i].at[block_rows(y, (z + 4 - (j + 1) * step_of(way)) % 4), :]
        return copy(part, part, wf_s.at[i - 4, way, j], wf_r.at[i - 4, way, j], yp)

    def w_send(i):
        if i < 4:
            for d in (2, 1, 3):
                wz_desc(i, d).start()
        else:
            for way in range(2):

                @pl.when(goes(way, 0))
                def _():
                    wc_desc(i, way, 0).start()

    def w_over(i):
        wy_desc(i, 0).start()

    def w_pass(i):
        for d in (2, 1, 3):
            wz_desc(i, d).wait_recv()
            wy_desc(i, d).start()

    def w_relay(i, j):
        for way in range(2):

            @pl.when(came(way, j))
            def _():
                wc_desc(i, way, j).wait_recv()

            if j < 2:

                @pl.when(goes(way, j + 1))
                def _():
                    wc_desc(i, way, j + 1).start()

            @pl.when(came(way, j))
            def _():
                wf_desc(i, way, j).start()

    def w_wait(i):
        wy_desc(i, 0).wait_recv()
        if i < 4:
            for d in (1, 2, 3):
                wy_desc(i, d).wait_recv()
            return
        for way in range(2):
            for j in range(3):

                @pl.when(came(way, j))
                def _():
                    wf_desc(i, way, j).wait_recv()

    for i in range(2):
        w_send(i)
        w_over(i)
    own = block_rows(y, z)
    for s in range(2):
        X[s, chunk(t), :] = x_ref[s]
        ag_start(0, X, s)
    w_send(2)
    w_over(2)
    TBR[...] = jnp.zeros_like(TBR)
    COMB[...] = jnp.zeros_like(COMB)
    GCOMB[...] = jnp.zeros_like(GCOMB)

    def seg_desc(d):
        return copy(seg_ref, SEGZ.at[z], seg_s.at[d - 1], seg_r.at[d - 1], along(d))

    for d in (1, 2, 3):
        seg_desc(d).start()
    WK[own, :] = wk_ref[...]
    WV[own, :] = wv_ref[...]
    WQ[own, :] = wq_ref[...]
    WU[own, :] = wu_ref[...]
    turned = wo_ref[...].T
    OWN_O[...] = turned
    WO[own, :] = turned
    WD[own, :] = wd_ref[...]

    def split_omega(h, carry):
        om = om_ref[h]
        hi = om.astype(BF)
        low = (om - hi.astype(F32)).astype(BF)
        zero = jnp.zeros((64, 256), BF)
        OM1[h] = jnp.concatenate([hi, zero, hi, zero], axis=0)
        OM2[h] = jnp.concatenate([low, zero], axis=0)
        turned = jnp.concatenate([om, jnp.zeros((64, 256), F32)], axis=0).T
        t_hi = turned.astype(BF)
        t_low = (turned - t_hi.astype(F32)).astype(BF)
        one_at = (lanes_of((256, 128)) == 64).astype(BF)
        OMT[h] = jnp.concatenate([t_hi + one_at, t_low], axis=1)
        return carry

    lax.fori_loop(0, 3, split_omega, 0)

    w_pass(0)
    ag_pass(0, X, 0)
    ag_pass(0, X, 1)
    w_pass(1)

    for d in (1, 2, 3):
        seg_desc(d).wait_recv()
    seg_row = [seg_ref[s : s + 1, :] for s in range(2)]

    def edge(s, side, dist):
        if side == 0:
            return SEGZ[(z + 4 - dist) % 4, s : s + 1, 255:256]
        return SEGZ[(z + dist) % 4, s : s + 1, 0:1]

    def reaches(side, dist):
        return z >= dist if side == 0 else z + dist <= 3

    for s in range(2):
        wide = jnp.broadcast_to(seg_row[s].astype(F32), (256, 256))
        col = wide.T
        MSK[s] = (wide == col).astype(F32)
        for side in range(2):
            near = (col[:, 0:128] == edge(s, side, 1).astype(F32)).astype(F32)
            CM[side, s] = jnp.where(reaches(side, 1), near, 0.0)

    def first_row(s):
        return (seg_row[s] == seg_row[s][:, 0:1]).astype(F32)

    def last_row(s):
        return (seg_row[s] == seg_row[s][:, 255:256]).astype(F32)

    def project_keys(s):
        rows = X[s]
        made_k = nn(rows, WK[...]) * HEAD_DIM ** (-0.25)
        made_v = nn(rows, WV[...])
        zero = jnp.zeros((256, 64), F32)
        lane = lanes_of((256, 128))
        for h in range(3):
            i = s * 3 + h
            RK[i] = jnp.concatenate([made_k[:, 64 * h : 64 * h + 64], zero], axis=1)
            v_h = jnp.concatenate([made_v[:, 64 * h : 64 * h + 64], zero], axis=1)
            VX[i] = jnp.where((lane == 64) | (lane == 65), 1.0, v_h).astype(BF)

    def project_queries(s):
        made_q = nn(X[s], WQ[...]) * HEAD_DIM ** (-0.25)
        zero = jnp.zeros((256, 64), F32)
        for h in range(3):
            RQ[s * 3 + h] = jnp.concatenate([made_q[:, 64 * h : 64 * h + 64], zero], axis=1)

    def phi_of(scaled, h):
        hi = scaled.astype(BF)
        low = (scaled - hi.astype(F32)).astype(BF)
        angles = nn(jnp.concatenate([hi, low], axis=1), OM1[h]) + nn(hi, OM2[h])
        squares = 0.5 * jnp.sum(scaled * scaled, -1, keepdims=True)
        return jnp.exp(angles - squares) * FEATS ** (-0.5)

    def tables(ext, feats, s):
        turned = ext.astype(F32).T[0:TAB, :]
        both = jnp.concatenate([turned * first_row(s), turned * last_row(s)], axis=0)
        return nn(both.astype(BF), feats)

    def keys(s):
        def body(h, carry):
            i = s * 3 + h
            phi = phi_of(RK[i], h)
            PKF[i] = phi
            low = phi.astype(BF)
            PK[i] = low
            made = tables(VX[i], low, s)
            TBS[0, 1, i] = made[0:TAB].astype(BF)
            TBS[0, 0, i] = made[TAB : 2 * TAB].astype(BF)
            return carry

        lax.fori_loop(0, 3, body, 0, unroll=True)

    def queries(s):
        def body(h, carry):
            i = s * 3 + h
            phi = phi_of(RQ[i], h)
            PQF[i] = phi
            low = phi.astype(BF)
            PQ[i] = low
            score = jnp.where(MSK[s] > 0, nt(low, PK[i]), 0.0).astype(BF)
            SS[i] = score
            MIX[i] = nn(score, VX[i])
            return carry

        lax.fori_loop(0, 3, body, 0, unroll=True)

    def mixing(s):
        tb_take(0, s, COMB)

        def body(h, carry):
            i = s * 3 + h
            cross = nt(PQ[i], COMB[i])
            numer = MIX[i] + jnp.where(CM[0, s] > 0, cross[:, 0:128], 0.0)
            numer = numer + jnp.where(CM[1, s] > 0, cross[:, 128:256], 0.0)
            denom = numer[:, 64:65]
            mixed = numer / denom
            MIX[i] = jnp.where(lanes_of((256, 128)) < 64, mixed, 0.0)
            DEN[i] = jnp.broadcast_to(denom, (256, 128))
            return carry

        lax.fori_loop(0, 3, body, 0, unroll=True)
        MIXC[s] = jnp.concatenate(
            [MIX[s * 3][:, 0:64], MIX[s * 3 + 1][:, 0:64], MIX[s * 3 + 2][:, 0:64]], axis=1
        ).astype(BF)

    def tb_desc(way, s, side, dist):
        heads = pl.ds(s * 3, 3)
        src = TBS.at[way, side, heads] if dist == 1 else TBR.at[way, side, 0, heads]
        return copy(
            src,
            TBR.at[way, side, dist - 1, heads],
            tb_s.at[way, s, side, dist - 1],
            tb_r.at[way, s, side, dist - 1],
            along(1 if side == 0 else 3),
        )

    def tb_send(way, s):
        for side in range(2):

            @pl.when(reaches(1 - side, 1))
            def _():
                tb_desc(way, s, side, 1).start()

    def tb_relay(way, s):
        for side in range(2):

            @pl.when(reaches(side, 1))
            def _():
                tb_desc(way, s, side, 1).wait_recv()

            @pl.when((z == 1) | (z == 2))
            def _():
                tb_desc(way, s, side, 2).start()

    def tb_take(way, s, comb):
        for side in range(2):

            @pl.when(reaches(side, 2))
            def _():
                tb_desc(way, s, side, 2).wait_recv()

            both = (edge(s, side, 1) == edge(s, side, 2)) & reaches(side, 2)
            both = jnp.broadcast_to(both, (TAB, 256))
            for h in range(3):
                i = s * 3 + h
                near = TBR[way, side, 0, i].astype(F32)
                total = near + jnp.where(both, TBR[way, side, 1, i].astype(F32), 0.0)
                comb[i, 128 * side : 128 * side + TAB, :] = total.astype(BF)

    def attn_out(s):
        P[s] = nt(MIXC[s], WO[...])

    gain_attn, shift_attn, gain_ffn, shift_ffn, bias_down = (
        ref[...].reshape(1, 768) for ref in (ga_ref, sa_ref, gf_ref, sf_ref, bd_ref)
    )
    ARS[0] = jnp.zeros((8, 768), F32)

    def add_small(row, value):
        ARS[0, row : row + 1, :] = ARS[0, row : row + 1, :] + value

    def over_rows(value):
        return jnp.sum(value, 0, keepdims=True)

    def norm_one(s, attn):
        normed, inv_std = norm_stats(x_ref[s].astype(F32) + attn)
        first = normed * gain_attn + shift_attn
        NORM1[s], FIRST[s] = normed, first
        INV1[s] = jnp.broadcast_to(inv_std, (64, 128))
        FI[s, chunk(t), :] = first.astype(BF)

    def norm_two(s, branch):
        normed, inv_std = norm_stats(FIRST[s] + branch + bias_down)
        out_ref[s] = (normed * gain_ffn + shift_ffn).astype(BF)
        cot = cot_ref[s].astype(F32)
        grad = norm_grad(cot, normed, inv_std, gain_ffn)
        GH2[s] = grad
        G2[s, chunk(t), :] = grad.astype(BF)
        add_small(2, over_rows(cot * normed))
        add_small(3, over_rows(cot))
        add_small(4, over_rows(grad))

    def norm_one_back(s, summed):
        grad_first = GH2[s] + summed
        normed = NORM1[s]
        grad = norm_grad(grad_first, normed, INV1[s][:, 0:1], gain_attn)
        GH1[s] = grad
        G1[s, chunk(t), :] = grad.astype(BF)
        add_small(0, over_rows(grad_first * normed))
        add_small(1, over_rows(grad_first))

    def tile(j):
        return pl.ds(pl.multiple_of(j * 256, 256), 256)

    def ffn_up(s):
        def body(j, carry):
            upper = nn(FI[s], WU[:, tile(j)]) + bu_ref[tile(j)].reshape(1, 256)
            cdf = 0.5 * (1.0 + lax.erf(upper * root_half))
            HID[s, :, tile(j)] = (upper * cdf).astype(BF)
            SLOPE[s, :, tile(j)] = cdf + upper * inv_root_tau * jnp.exp(-0.5 * upper * upper)
            return carry

        lax.fori_loop(0, 3, body, 0, unroll=True)

    def ffn_down(s):
        def body(j, carry):
            P[s, :, tile(j)] = nt(HID[s], WD[tile(j), :])
            return carry

        lax.fori_loop(0, 3, body, 0, unroll=True)

    def ffn_back_hidden(s):
        def body(j, carry):
            grad = (nn(G2[s], WD[:, tile(j)]) * SLOPE[s, :, tile(j)]).astype(BF)
            GUP[s, :, tile(j)] = grad
            ARS[0, 5:6, tile(j)] = ARS[0, 5:6, tile(j)] + over_rows(grad.astype(F32))
            return carry

        lax.fori_loop(0, 3, body, 0, unroll=True)

    def ffn_back_rows(s):
        def body(j, carry):
            P[s, :, tile(j)] = nt(GUP[s], WU[tile(j), :])
            return carry

        lax.fori_loop(0, 3, body, 0, unroll=True)

    def slots(i):
        narrow, wide = (GON, YSN, YRN, ZSN, ZRN), (GOW, YSW, YRW, ZSW, ZRW)
        return [ref.at[i] for ref in narrow] if i < 4 else [ref.at[i - 4] for ref in wide]

    def half_lanes(yy, j):
        return pl.ds(pl.multiple_of(yy * 384 + j * 128, 128), 128)

    def weight_part(left, right, yy, j):
        lanes = half_lanes(yy, j)
        return tn(left[0, :, lanes], right[0]) + tn(left[1, :, lanes], right[1])

    def half_rows(j):
        return pl.ds(pl.multiple_of(j * 128, 128), 128)

    def weight_send(i, left, right):
        sent = slots(i)[1]

        def other(j, carry):
            sent[half_rows(j), :] = weight_part(left, right, 1 - y, j).astype(BF)
            return carry

        lax.fori_loop(0, 3, other, 0)
        for n in range(4):
            block = (z + (2, 1, 3, 0)[n]) % 4 if i < 4 else n + (1 - z // 2) * (3 - 2 * n)
            gy_desc(i, block).start()

    def weight_keep(i, left, right):
        own_half = slots(i)[0]

        def here(j, carry):
            own_half[half_rows(j), :] = weight_part(left, right, y, j)
            return carry

        lax.fori_loop(0, 3, here, 0)

    def z_rows(block):
        return pl.ds(pl.multiple_of(block * 96, 96), 96)

    def gy_desc(i, block):
        sent, came_y = slots(i)[1:3]
        return copy(sent.at[z_rows(block), :], came_y.at[block], gy_s.at[i, block], gy_r.at[i, block], yp)

    def gz_desc(i, d):
        sent, came_z = slots(i)[3:5]
        return copy(sent.at[d - 1], came_z.at[d - 1], gz_s.at[i, d - 1], gz_r.at[i, d - 1], along(d))

    def chip_sum(i, block):
        own_half, _, came_y, _, _ = slots(i)
        gy_desc(i, block).wait_recv()
        return own_half[z_rows(block), :] + came_y[block].astype(F32)

    def g_pass(i):
        sent = slots(i)[3]
        for d in (2, 1, 3):
            sent[d - 1] = chip_sum(i, (z + d) % 4).astype(BF)
            gz_desc(i, d).start()

    def gc_desc(i, way, e):
        sent, came_z = ZSW.at[i - 4, way, e], ZRW.at[i - 4, way, e]
        return copy(sent, came_z, gc_s.at[i - 4, way, e], gc_r.at[i - 4, way, e], along(4 + step_of(way)))

    def gives(way, e):
        return z + e < 3 if way == 0 else z > e

    def behind(way):
        return z > 0 if way == 0 else z < 3

    def g_relay(i, e):
        for way in range(2):

            @pl.when(gives(way, e))
            def _():
                total = chip_sum(i, (z + 4 + (e + 1) * step_of(way)) % 4)
                ZSW[i - 4, way, e] = total.astype(BF)
                if e < 2:

                    @pl.when(behind(way))
                    def _():
                        gc_desc(i, way, e + 1).wait_recv()
                        ZSW[i - 4, way, e] = (total + ZRW[i - 4, way, e + 1].astype(F32)).astype(BF)

                gc_desc(i, way, e).start()

    def g_last(i, out):
        total = chip_sum(i, z)
        if i < 4:
            arrived = slots(i)[4]
            for d in (1, 2, 3):
                gz_desc(i, d).wait_recv()
                total = total + arrived[d - 1].astype(F32)
            out[...] = total
            return
        out[...] = total
        for way in range(2):

            @pl.when(behind(way))
            def _():
                gc_desc(i, way, 0).wait_recv()
                out[...] = out[...] + ZRW[i - 4, way, 0].astype(F32)

    def ar_desc(stage):
        where = (sib, far, yp)[stage]
        return copy(ARS.at[stage], ARR.at[stage], ar_s.at[stage], ar_r.at[stage], where)

    def ar_take(stage):
        ar_desc(stage).wait_recv()
        came = ARR[stage]
        if stage < 2:
            rows = lax.broadcasted_iota(jnp.int32, (8, 768), 0)
            came = jnp.where(rows < 5, came, 0.0)
        ARS[stage + 1] = ARS[stage] + came

    def ar_z_desc(i):
        return copy(ARS.at[3], ARZ.at[z], ar_s.at[3 + i], ar_r.at[3 + i], along(1 + i))

    def ar_z_start():
        ARZ[z] = ARS[3]
        for i in range(3):
            ar_z_desc(i).start()

    def ar_z_take():
        for i in range(3):
            ar_z_desc(i).wait_recv()
        small_ref[...] = (ARZ[0] + ARZ[1]) + (ARZ[2] + ARZ[3])

    def grad_tables(s):
        GM[...] = nn(G1[s], WO[...])
        lane = lanes_of((256, 128))
        zero = jnp.zeros((256, 64), F32)
        for h in range(3):
            i = s * 3 + h
            gm = jnp.concatenate([GM[:, 64 * h : 64 * h + 64], zero], axis=1)
            denom = DEN[i]
            slope = -jnp.sum(gm * MIX[i], -1, keepdims=True) / denom
            s_hi = slope.astype(BF).astype(F32)
            ext = jnp.where(lane == 64, s_hi, gm / denom)
            GX[i] = jnp.where(lane == 65, slope - s_hi, ext).astype(BF)

        def body(h, carry):
            i = s * 3 + h
            made = tables(GX[i], PQ[i], s)
            TBS[1, 1, i] = made[0:TAB].astype(BF)
            TBS[1, 0, i] = made[TAB : 2 * TAB].astype(BF)
            return carry

        lax.fori_loop(0, 3, body, 0, unroll=True)

    def pair(ext, s):
        ext = ext.astype(F32)
        return jnp.concatenate([ext * CM[0, s], ext * CM[1, s]], axis=1).astype(BF)

    def through_phi(grad_phi, phi, scaled, h):
        both = nn((grad_phi * phi).astype(BF), OMT[h])
        both = both[:, 0:128] + both[:, 128:256]
        return (both - scaled * both[:, 64:65]) * HEAD_DIM ** (-0.25)

    def side_by_side(heads):
        return jnp.concatenate([heads[h][:, 0:64] for h in range(3)], axis=1).astype(BF)

    def back_queries(s):
        def body(h, carry):
            i = s * 3 + h
            ext = GX[i]
            pairs = jnp.where(MSK[s] > 0, nt(ext, VX[i]), 0.0).astype(BF)
            grad = nn(pairs, PK[i]) + nn(pair(ext, s), COMB[i])
            GM3[h] = through_phi(grad, PQF[i], RQ[i], h)
            GKL[i] = tn(pairs, PQ[i])
            GVL[i] = tn(SS[i], ext)
            return carry

        lax.fori_loop(0, 3, body, 0, unroll=True)
        RGQ[s] = side_by_side(GM3)

    def back_keys(s):
        tb_take(1, s, GCOMB)

        def body(h, carry):
            i = s * 3 + h
            grad = GKL[i] + nn(pair(VX[i], s), GCOMB[i])
            GM3[h] = through_phi(grad, PKF[i], RK[i], h)
            cross = nt(PK[i], GCOMB[i])
            gv = GVL[i] + jnp.where(CM[0, s] > 0, cross[:, 0:128], 0.0)
            GV3[h] = gv + jnp.where(CM[1, s] > 0, cross[:, 128:256], 0.0)
            return carry

        lax.fori_loop(0, 3, body, 0, unroll=True)
        RGK[s] = side_by_side(GM3)
        RGV[s] = side_by_side(GV3)

    def input_rows(s):
        def body(j, carry):
            made = nt(RGQ[s], WQ[tile(j), :]) + nt(RGK[s], WK[tile(j), :])
            P[s, :, tile(j)] = made + nt(RGV[s], WV[tile(j), :])
            return carry

        lax.fori_loop(0, 3, body, 0, unroll=True)

    w_send(4)
    w_send(3)
    w_send(5)
    w_pass(2)
    w_over(3)
    w_over(4)
    w_over(5)
    w_wait(0)
    w_wait(1)
    ag_wait(0, X, 0)
    project_keys(0)
    keys(0)
    tb_send(0, 0)
    ag_wait(0, X, 1)
    project_keys(1)
    keys(1)
    tb_send(0, 1)
    w_pass(3)
    w_wait(2)
    project_queries(0)
    queries(0)
    tb_relay(0, 0)
    project_queries(1)
    queries(1)
    tb_relay(0, 1)
    w_relay(4, 0)
    w_relay(5, 0)
    mixing(0)
    w_wait(3)
    attn_out(0)
    rs_start(0, 0)
    mixing(1)
    attn_out(1)
    rs_mid(0, 0)
    rs_start(0, 1)
    w_relay(4, 1)
    rs_mid(0, 1)
    norm_one(0, rs_fin(0, 0))
    ag_start(1, FI, 0)
    w_relay(5, 1)
    norm_one(1, rs_fin(0, 1))
    ag_start(1, FI, 1)
    w_relay(4, 2)
    ag_pass(1, FI, 0)
    ag_wait(1, FI, 0)
    w_relay(5, 2)
    w_wait(4)
    ffn_up(0)
    ag_pass(1, FI, 1)
    w_wait(5)
    ffn_down(0)
    rs_start(1, 0)
    ag_wait(1, FI, 1)
    ffn_up(1)
    rs_mid(1, 0)
    ffn_down(1)
    rs_start(1, 1)
    rs_mid(1, 1)
    norm_two(0, rs_fin(1, 0))
    ag_start(2, G2, 0)
    norm_two(1, rs_fin(1, 1))
    ag_start(2, G2, 1)
    ag_pass(2, G2, 0)
    ag_wait(2, G2, 0)
    ffn_back_hidden(0)
    ag_pass(2, G2, 1)
    ffn_back_rows(0)
    rs_start(2, 0)
    ag_wait(2, G2, 1)
    weight_send(5, G2, HID)
    rs_mid(2, 0)
    ffn_back_hidden(1)
    ffn_back_rows(1)
    rs_start(2, 1)
    weight_send(4, FI, GUP)
    rs_mid(2, 1)
    norm_one_back(0, rs_fin(2, 0))
    ag_start(3, G1, 0)
    weight_keep(5, G2, HID)
    norm_one_back(1, rs_fin(2, 1))
    ag_start(3, G1, 1)
    ar_desc(0).start()
    g_relay(5, 2)
    ag_pass(3, G1, 0)
    weight_keep(4, FI, GUP)
    ag_wait(3, G1, 0)
    grad_tables(0)
    tb_send(1, 0)
    ag_pass(3, G1, 1)
    ar_take(0)
    ar_desc(1).start()
    ag_wait(3, G1, 1)
    grad_tables(1)
    tb_send(1, 1)
    ar_take(1)
    ar_desc(2).start()
    weight_send(3, G1, MIXC)
    g_relay(5, 1)
    back_queries(0)
    tb_relay(1, 0)
    back_queries(1)
    g_relay(4, 2)
    tb_relay(1, 1)
    weight_send(2, X, RGQ)
    weight_keep(3, G1, MIXC)
    weight_keep(2, X, RGQ)
    g_relay(5, 0)
    back_keys(0)
    input_rows(0)
    rs_start(3, 0)
    back_keys(1)
    rs_mid(3, 0)
    weight_send(0, X, RGK)
    weight_send(1, X, RGV)
    g_relay(4, 1)
    input_rows(1)
    rs_start(3, 1)
    weight_keep(0, X, RGK)
    weight_keep(1, X, RGV)
    ar_take(2)
    ar_z_start()
    g_pass(3)
    rs_mid(3, 1)
    g_pass(2)
    g_relay(4, 0)
    g_pass(0)
    g_pass(1)
    gin_ref[0] = (GH1[0] + rs_fin(3, 0)).astype(BF)
    gin_ref[1] = (GH1[1] + rs_fin(3, 1)).astype(BF)
    ar_z_take()
    g_last(5, od_ref)
    g_last(4, ou_ref)
    g_last(3, oo_ref)
    g_last(2, oq_ref)
    g_last(0, ok_ref)
    g_last(1, ov_ref)

    for s in range(2):
        for op, buf in enumerate((X, FI, G2, G1)):
            for which in range(3):
                ag_desc(op, buf, s, which).wait_send()
        for op in range(4):
            sib_desc(op, s, 0).wait_send()
            sib_desc(op, s, 1).wait_send()
            xrs_desc(op, s).wait_send()
        for way in range(2):
            for side in range(2):

                @pl.when(reaches(1 - side, 1))
                def _():
                    tb_desc(way, s, side, 1).wait_send()

                @pl.when((z == 1) | (z == 2))
                def _():
                    tb_desc(way, s, side, 2).wait_send()

    for i in range(6):
        wy_desc(i, 0).wait_send()
        for block in range(4):
            gy_desc(i, block).wait_send()
        for d in (1, 2, 3):
            if i < 4:
                wy_desc(i, d).wait_send()
                wz_desc(i, d).wait_send()
                gz_desc(i, d).wait_send()
    for i in (4, 5):
        for way in range(2):
            for j in range(3):

                @pl.when(goes(way, j))
                def _():
                    wc_desc(i, way, j).wait_send()

                @pl.when(came(way, j))
                def _():
                    wf_desc(i, way, j).wait_send()

                @pl.when(gives(way, j))
                def _():
                    gc_desc(i, way, j).wait_send()

    for stage in range(3):
        ar_desc(stage).wait_send()
        ar_z_desc(stage).wait_send()
        seg_desc(stage + 1).wait_send()


def hand_out(
    out_ref, gin_ref, ok_ref, ov_ref, oq_ref, oo_ref, ou_ref, od_ref, small_ref,
    out_o, gin_o, q_o, k_o, v_o, o_o, ga_o, sa_o, u_o, bu_o, d_o, bd_o, gf_o, sf_o,
):
    narrow = ((q_o, oq_ref), (k_o, ok_ref), (v_o, ov_ref))
    for dst, src in narrow + ((out_o, out_ref), (gin_o, gin_ref), (u_o, ou_ref), (d_o, od_ref)):
        dst[...] = src[...]
    o_o[...] = oo_ref[...].T
    for row, dst in enumerate((ga_o, sa_o, gf_o, sf_o, bd_o, bu_o)):
        dst[...] = small_ref[row, :]


def dma(*shape):
    return pltpu.SemaphoreType.DMA(shape)


def fast_device(
    inputs, seg_ids, feature_map, w_query, w_key, w_value, w_out, gain_attn, shift_attn,
    w_up, bias_up, w_down, bias_down, gain_ffn, shift_ffn, cotangent,
):
    vm = pltpu.VMEM
    scratch = [
        vm((2, 256, 768), BF), vm((2, 256, 768), BF), vm((2, 256, 768), BF), vm((2, 256, 768), BF),
        vm((768, 192), BF), vm((768, 192), BF), vm((768, 192), BF), vm((768, 192), BF),
        vm((768, 768), BF), vm((768, 768), BF), vm((96, 192), BF),
        vm((2, 256, 768), F32), vm((2, 256, 768), BF), vm((2, 256, 768), F32), vm((2, 256, 768), BF),
        vm((2, 64, 768), F32), vm((2, 64, 768), F32), vm((2, 64, 128), F32),
        vm((2, 64, 768), F32), vm((2, 64, 768), F32),
        vm((6, 256, 128), F32), vm((6, 256, 128), F32), vm((6, 256, 128), BF),
        vm((6, 256, 256), F32), vm((6, 256, 256), F32), vm((6, 256, 256), BF), vm((6, 256, 256), BF),
        vm((6, 256, 256), BF),
        vm((2, 256, 256), F32), vm((2, 2, 256, 128), F32), vm((4, 2, 256), jnp.int32),
        vm((3, 256, 256), BF), vm((3, 128, 256), BF), vm((3, 256, 256), BF),
        vm((6, 256, 128), F32), vm((6, 256, 128), F32), vm((6, 256, 128), BF),
        vm((6, 256, 256), F32), vm((6, 256, 128), F32),
        vm((256, 192), F32), vm((3, 256, 128), F32), vm((3, 256, 128), F32),
        vm((2, 256, 192), BF), vm((2, 256, 192), BF), vm((2, 256, 192), BF), vm((2, 256, 192), BF),
        vm((2, 2, 6, TAB, 256), BF), vm((2, 2, 2, 6, TAB, 256), BF), vm((6, 256, 256), BF), vm((6, 256, 256), BF),
        vm((4, 2, 2, 64, 768), BF), vm((4, 2, 2, 64, 768), BF), vm((4, 2, 64, 768), BF), vm((4, 2, 64, 768), BF),
        vm((4, 384, 192), F32), vm((2, 384, 768), F32),
        vm((4, 384, 192), BF), vm((2, 384, 768), BF),
        vm((4, 4, 96, 192), BF), vm((2, 4, 96, 768), BF),
        vm((4, 3, 96, 192), BF), vm((2, 2, 3, 96, 768), BF),
        vm((4, 3, 96, 192), BF), vm((2, 2, 3, 96, 768), BF),
        vm((4, 8, 768), F32), vm((3, 8, 768), F32), vm((4, 8, 768), F32),
        dma(4, 2, 3), dma(4, 2, 3), dma(4, 2, 3), dma(4, 2, 3), dma(3), dma(3),
        dma(4, 3), dma(4, 3), dma(6, 4), dma(6, 4), dma(2, 2, 3), dma(2, 2, 3), dma(2, 2, 3), dma(2, 2, 3),
        dma(6, 4), dma(6, 4), dma(4, 3), dma(4, 3), dma(2, 2, 3), dma(2, 2, 3),
        dma(2, 2, 2, 2), dma(2, 2, 2, 2), dma(6), dma(6),
    ]
    in_vmem = pl.BlockSpec(memory_space=pltpu.VMEM)
    shape = jax.ShapeDtypeStruct
    narrow, wide, rows, vec = shape((96, 192), F32), shape((96, 768), F32), shape((2, 64, 768), BF), shape((768,), F32)
    made = pl.pallas_call(
        layer_kernel,
        out_shape=(rows, rows, narrow, narrow, narrow, narrow, wide, wide, shape((8, 768), F32)),
        in_specs=[in_vmem] * 16,
        out_specs=(in_vmem,) * 9,
        scratch_shapes=scratch,
        compiler_params=pltpu.CompilerParams(
            collective_id=0, has_side_effects=True, vmem_limit_bytes=67043328
        ),
    )(
        inputs, seg_ids, feature_map, w_query, w_key, w_value, w_out, gain_attn, shift_attn,
        w_up, bias_up, w_down.T, bias_down, gain_ffn, shift_ffn, cotangent,
    )
    done = pl.pallas_call(
        hand_out,
        out_shape=(
            rows, rows, narrow, narrow, narrow, shape((192, 96), F32), vec, vec,
            wide, vec, wide, vec, vec, vec,
        ),
        in_specs=[in_vmem] * 9,
        out_specs=(in_vmem,) * 14,
    )(*made)
    return (*done[:10], done[10].T, *done[11:])


def solution(mesh):
    placed = (
        P("shard", ("ctx", "tp"), None),
        P("shard", "ctx"),
        P("tp", None, None),
        P(("shard", "ctx"), "tp"),
        P(("shard", "ctx"), "tp"),
        P(("shard", "ctx"), "tp"),
        P("tp", ("shard", "ctx")),
        P(),
        P(),
        P(("shard", "ctx"), "tp"),
        P("tp"),
        P("tp", ("shard", "ctx")),
        P(),
        P(),
        P(),
        P("shard", ("ctx", "tp"), None),
    )
    sizes = tuple(mesh.shape[axis] for axis in ("shard", "ctx", "tp"))
    return jax.shard_map(
        fast_device if sizes == (2, 4, 4) else per_device,
        mesh=mesh,
        in_specs=placed,
        out_specs=(
            P("shard", ("ctx", "tp"), None),
            P("shard", ("ctx", "tp"), None),
            P(("shard", "ctx"), "tp"),
            P(("shard", "ctx"), "tp"),
            P(("shard", "ctx"), "tp"),
            P("tp", ("shard", "ctx")),
            P(),
            P(),
            P(("shard", "ctx"), "tp"),
            P("tp"),
            P("tp", ("shard", "ctx")),
            P(),
            P(),
            P(),
        ),
        check_vma=False,
    )
```
